512 devices in a mesh: seq: 64 (over z, x, core), fsdp: 8 (over y).
Axes of the slice: x: 4, y: 8, z: 8, core: 2. Of those that a mesh axis runs over, the one named last changes fastest.
Arguments:
- queries: bfloat16 [8, 8192, 1536], P('fsdp', 'seq'), may hold values from -6 to 6
- keys: bfloat16 [8, 8192, 1536], P('fsdp', 'seq'), may hold values from -6 to 6
- values: bfloat16 [8, 8192, 1536], P('fsdp', 'seq'), may hold values from -27.2 to 27.2
- lengths: int32 [8, 16], P('fsdp'), may hold values from 1 to 1024, 8192 in all within a row
- gain: float32 [1536], replicated, may hold values from 0.5 to 2
- out_weight: bfloat16 [1536, 2048], P('fsdp'), may hold values from -0.15625 to 0.15625
- cotangent: bfloat16 [8, 8192, 2048], P('fsdp', 'seq'), may hold values from -6 to 6
Outputs:
- output: bfloat16 [8, 8192, 2048], P('fsdp', 'seq')
- grad_queries: bfloat16 [8, 8192, 1536], P('fsdp', 'seq')
- grad_keys: bfloat16 [8, 8192, 1536], P('fsdp', 'seq')
- grad_values: bfloat16 [8, 8192, 1536], P('fsdp', 'seq')
The draws below stay inside these ranges and needn't reach their ends.
Inputs may be any that keep to these rules, and one draw needn't show every extreme that they name: Each row holds the lengths of the documents packed into one sequence, in order; a row sums to 8192 and its longest document has exactly 1024 positions.
All inputs are finite; a program needn't handle non-finite values.
Results may differ from the reference program's by a relative error of at most 0.012.
Values may be sent and summed in bfloat16 or wider, within the bound.
No kernel may reach another device: no remote copies, remote signals or barrier semaphores. Data moves between devices by JAX's collectives and lax.ppermute only.
A program may use at most 128 MiB of HBM per device.

```python
import math
import jax
import jax.numpy as jnp
import numpy as np
from jax import lax

D = 2048
HEADS = 12
HEAD_DIM = 128
NDOCS = 16
TOK_DEV = 128
DI = 1536
LENGTH = 8192
SEQS = 8
MOST = 1024


def draw_values(key, part):
    key_noise = jax.random.fold_in(key, 11)
    key_column = jax.random.fold_in(key, 12)
    column_scale = jnp.exp(jax.random.uniform(key_column, (DI,), jnp.float32, 0.0, math.log(10.0))) * 0.4
    noise_field = jnp.clip(jax.random.normal(key_noise, (SEQS, LENGTH, DI), jnp.float32), -5.0, 5.0)
    return (noise_field * column_scale).astype(jnp.bfloat16)


def level_of(key, extent, cuts, smallest, largest):
    level = 1.0
    for position, shards_of in cuts:
        draws = jax.random.uniform(jax.random.fold_in(jax.random.fold_in(key, 6), position), (shards_of,), jnp.float32, smallest / len(cuts), largest / len(cuts))
        level = level * jnp.repeat(jnp.exp(draws), extent[position] // shards_of).reshape((-1,) + (1,) * (len(extent) - 1 - position))
    return level


def split_up(amount, total, reach, lean):
    loads = [(1 << 20) // math.isqrt(rank ** lean) + 1 for rank in range(2, amount + 1)]
    rest, holding = total - reach - (amount - 1), [1] * (amount - 1)
    while rest > 0:
        free = [i for i in range(amount - 1) if holding[i] < reach]
        pool, remaining = sum([loads[i] for i in free]), rest
        for i in free:
            extra = min(reach - holding[i], max(1, remaining * loads[i] // pool), rest)
            holding[i] = holding[i] + extra
            rest = rest - extra
    return np.array([reach] + holding)


def uneven_parts(stream_key, count, total, reach, skew):
    if count == 2:
        one = jax.random.randint(stream_key, (), max(1, total - reach), min(reach, total - 1) + 1)
        return jnp.stack([one, total - one])
    sizes = jnp.asarray(split_up(count, total, reach, skew), jnp.int32)
    pairs = (count - 1) // 2
    donor, sink = sizes[1:1 + 2 * pairs:2], sizes[2:2 + 2 * pairs:2]
    slack = jnp.minimum(donor - 1, reach - sink)
    passed = jax.random.randint(jax.random.fold_in(stream_key, 1), (pairs,), 0, 1 << 20) % (slack + 1)
    sizes = sizes.at[1:1 + 2 * pairs:2].set(donor - passed).at[2:2 + 2 * pairs:2].set(sink + passed)
    return sizes[jax.random.permutation(jax.random.fold_in(stream_key, 2), count)]


def noise(stream_key, shape, width, most, shards=(), kind=jnp.bfloat16):
    drawn = jax.random.normal(stream_key, shape, jnp.float32) * width
    if len(shards) > 0:
        drawn = level_of(stream_key, shape, shards, -0.22, 0.18) * drawn
    return jnp.clip(drawn, min=-most, max=most).astype(kind)


def setup_inputs(seed: int = 0) -> dict:
    splits = jax.random.split(jax.random.key(seed), 8)
    return {
        "queries": noise(splits[0], (SEQS, LENGTH, DI), 1.0, 6.0, ((0, 8), (1, 64))),
        "keys": noise(splits[1], (SEQS, LENGTH, DI), 1.0, 6.0, ((0, 8), (1, 64))),
        "values": draw_values(jax.random.fold_in(splits[7], 71), 0),
        "lengths": jax.vmap(lambda own: uneven_parts(own, NDOCS, LENGTH, MOST, 1))(jax.random.split(splits[3], SEQS)).reshape((SEQS, NDOCS)).astype(jnp.int32),
        "gain": jnp.clip(jnp.exp(jax.random.uniform(splits[4], (DI,), jnp.float32, math.log(0.5), math.log(2.0))), 0.5, 2.0),
        "out_weight": noise(splits[5], (DI, D), DI ** -0.5, 0.15625, ((0, 8),)),
        "cotangent": noise(splits[6], (SEQS, LENGTH, D), 1.0, 6.0, ((0, 8), (1, 64))),
    }


epsilon = 1.0

def doc_index(doc_ends, positions):
    return lax.optimization_barrier(jnp.sum((doc_ends[None, :] <= positions[:, None]).astype(jnp.int32), axis=1))

def one_sequence(query_seq, key_seq, value_seq, length_row, gain, out_weight, cotangent_seq):
    blocks = LENGTH // TOK_DEV
    doc_ends = jnp.cumsum(length_row).astype(jnp.int32)
    offsets = jnp.arange(TOK_DEV, dtype=jnp.int32)
    causal = offsets[:, None] >= offsets[None, :]
    query_blk = query_seq.reshape(blocks, TOK_DEV, HEADS, HEAD_DIM)
    key_blk = key_seq.reshape(blocks, TOK_DEV, HEADS, HEAD_DIM)
    value_blk = value_seq.reshape(blocks, TOK_DEV, HEADS, HEAD_DIM)
    numbers = jnp.arange(blocks, dtype=jnp.int32)

    def block_info(number):
        block_start = number * TOK_DEV
        doc_ids = doc_index(doc_ends, block_start + offsets)
        border = doc_index(doc_ends, jnp.stack([block_start - 1, block_start + TOK_DEV]).astype(jnp.int32))
        same_doc = causal & (doc_ids[:, None] == doc_ids[None, :])
        return (doc_ids, border[0], border[1], same_doc)

    def forward_step(state, inputs):
        number, query_part, key_part, value_part = inputs
        doc_ids, doc_before, doc_after, same_doc = block_info(number)
        query_f = query_part.astype(jnp.float32)
        key_f = key_part.astype(jnp.float32)
        value_f = value_part.astype(jnp.float32)
        scores = jnp.einsum('thd,shd->hts', query_f, key_f)
        attn_low = jnp.where(same_doc[None], scores, 0.0).astype(jnp.bfloat16)
        state_low = state.astype(jnp.bfloat16).astype(jnp.float32)
        inside = jnp.einsum('hts,shd->thd', attn_low.astype(jnp.float32), value_f)
        carried = jnp.einsum('thd,hde->the', query_f, state_low)
        mixed = inside + jnp.where((doc_ids == doc_before)[:, None, None], carried, 0.0)
        doc_last = doc_ids[TOK_DEV - 1]
        tail_values = jnp.where((doc_ids == doc_last)[:, None, None], value_f, 0.0)
        local_state = jnp.einsum('shd,she->hde', key_f, tail_values)
        new_state = jnp.where(doc_last != doc_before, local_state, local_state + state)
        return (new_state, (mixed, state))
    start_state = jnp.zeros((HEADS, HEAD_DIM, HEAD_DIM), jnp.float32)
    _, (mixed, states) = lax.scan(forward_step, start_state, (numbers, query_blk, key_blk, value_blk))
    mixed = mixed.reshape(LENGTH, HEADS, HEAD_DIM)
    inv_rms = lax.rsqrt(lax.optimization_barrier(jnp.mean(mixed * mixed, axis=-1, keepdims=True)) + epsilon)
    normed = mixed * inv_rms
    gain_heads = gain.reshape(HEADS, HEAD_DIM)
    scaled = (normed * gain_heads).astype(jnp.bfloat16).reshape(LENGTH, DI)
    output = jnp.dot(scaled, out_weight, preferred_element_type=jnp.float32).astype(jnp.bfloat16)
    grad_scaled = jnp.dot(cotangent_seq, out_weight.T, preferred_element_type=jnp.float32)
    grad_norm = grad_scaled.reshape(LENGTH, HEADS, HEAD_DIM) * gain_heads
    grad_mixed = inv_rms * (grad_norm - normed * lax.optimization_barrier(jnp.mean(grad_norm * normed, axis=-1, keepdims=True)))
    grad_blk = grad_mixed.astype(jnp.bfloat16).reshape(blocks, TOK_DEV, HEADS, HEAD_DIM)

    def backward_step(back_state, inputs):
        number, query_part, key_part, value_part, grad_part, state = inputs
        doc_ids, doc_before, doc_after, same_doc = block_info(number)
        query_f = query_part.astype(jnp.float32)
        key_f = key_part.astype(jnp.float32)
        value_f = value_part.astype(jnp.float32)
        grad_f = grad_part.astype(jnp.float32)
        scores = jnp.einsum('thd,shd->hts', query_f, key_f)
        attn_low = jnp.where(same_doc[None], scores, 0.0).astype(jnp.bfloat16).astype(jnp.float32)
        grad_attn = jnp.where(same_doc[None], jnp.einsum('thd,shd->hts', grad_f, value_f), 0.0)
        grad_attn = grad_attn.astype(jnp.bfloat16).astype(jnp.float32)
        state_low = state.astype(jnp.bfloat16).astype(jnp.float32)
        back_low = back_state.astype(jnp.bfloat16).astype(jnp.float32)
        carry_rows = (doc_ids == doc_before)[:, None, None]
        after_rows = (doc_ids == doc_after)[:, None, None]
        grad_query = jnp.einsum('hts,shd->thd', grad_attn, key_f)
        grad_query = grad_query + jnp.where(carry_rows, jnp.einsum('the,hde->thd', grad_f, state_low), 0.0)
        grad_key = jnp.einsum('hts,thd->shd', grad_attn, query_f)
        grad_key = grad_key + jnp.where(after_rows, jnp.einsum('she,hde->shd', value_f, back_low), 0.0)
        grad_value = jnp.einsum('hts,thd->shd', attn_low, grad_f)
        grad_value = grad_value + jnp.where(after_rows, jnp.einsum('shd,hde->she', key_f, back_low), 0.0)
        doc_first = doc_ids[0]
        head_queries = jnp.where((doc_ids == doc_first)[:, None, None], query_f, 0.0)
        local_state = jnp.einsum('thd,the->hde', head_queries, grad_f)
        new_state = jnp.where(doc_first != doc_after, local_state, local_state + back_state)
        return (new_state, (grad_query.astype(jnp.bfloat16), grad_key.astype(jnp.bfloat16), grad_value.astype(jnp.bfloat16)))
    _, (grad_query, grad_key, grad_value) = lax.scan(backward_step, start_state, (numbers, query_blk, key_blk, value_blk, grad_blk, states), reverse=True)
    return (output, grad_query.reshape(LENGTH, DI), grad_key.reshape(LENGTH, DI), grad_value.reshape(LENGTH, DI))

def reference(queries, keys, values, lengths, gain, out_weight, cotangent):

    def single(items):
        return one_sequence(items[0], items[1], items[2], items[3], gain, out_weight, items[4])
    output, grad_queries, grad_keys, grad_values = lax.map(single, (queries, keys, values, lengths, cotangent))
    return (output, grad_queries, grad_keys, grad_values)
```

```python
import jax
import jax.numpy as jnp
from jax import lax
from jax.experimental import pallas as pl
from jax.experimental.pallas import tpu as pltpu
from jax.sharding import Mesh, PartitionSpec as P


HEADS = 12
HALF = 6
HEAD_DIM = 128
NDOCS = 16
TOK = 128
DI = HEADS * HEAD_DIM
D = 2048
CHIPS = 32
EPSILON = 1.0
F32 = jnp.float32
BF16 = jnp.bfloat16

CA, CB, MP, ME1, ME3, CS, ES, CR, ER = range(9)
BACK = 9
ROWS = 24

VMEM = pl.BlockSpec(memory_space=pltpu.VMEM)
SMEM = pl.BlockSpec(memory_space=pltpu.SMEM)


def params(mib=24):
    return pltpu.CompilerParams(vmem_limit_bytes=mib << 20)


def cost(flops, moved):
    return pl.CostEstimate(flops=flops, bytes_accessed=moved, transcendentals=0)


def chip_and_core():
    return lax.axis_index("z") * 4 + lax.axis_index("x"), lax.axis_index("core")


def running_ends(lengths_ref):
    ends, total = [], jnp.int32(0)
    for j in range(NDOCS):
        total = total + lengths_ref[0, j]
        ends.append(total)
    return ends


def last_end(ends, position):
    best = jnp.int32(-(1 << 30))
    for end in ends:
        best = jnp.where(end <= position, end, best)
    return best


def next_end(ends, position):
    best = jnp.int32(1 << 30)
    for end in reversed(ends):
        best = jnp.where(end > position, end, best)
    return best


def same(ends, early, late):
    return last_end(ends, late) <= early


def lanes(head):
    start = head * HEAD_DIM
    return pl.ds(start if isinstance(head, int) else pl.multiple_of(start, HEAD_DIM), HEAD_DIM)


def dot(a, b, contract):
    return lax.dot_general(a, b, ((contract[0], contract[1]), ((), ())), preferred_element_type=F32)


NN = ((1,), (0,))
NT = ((1,), (1,))
TN = ((0,), (0,))


def rows_of(start, width=HEAD_DIM):
    return start + lax.broadcasted_iota(jnp.int32, (TOK, width), 0)


def same_doc_mask(ends, start):
    rows = rows_of(start)
    columns = start + lax.broadcasted_iota(jnp.int32, (TOK, TOK), 1)
    first = jnp.full((TOK, TOK), -(1 << 30), jnp.int32)
    for end in ends:
        first = jnp.where(end <= rows, end, first)
    return (columns <= rows) & (columns >= first)


def local_state_kernel(lengths_ref, keys_ref, values_ref, keep_ref, give_ref, coef_ref):
    chip, core = chip_and_core()
    ends = running_ends(lengths_ref)
    start = (chip * 2 + core) * TOK
    tail = rows_of(start) >= last_end(ends, start + TOK - 1)
    for part, ref in ((0, keep_ref), (1, give_ref)):
        first = HALF * core if part == 0 else HALF * (1 - core)
        for j in range(HALF):
            span = lanes(first + j)
            tail_values = jnp.where(tail, values_ref[:, span], 0)
            ref[j] = dot(keys_ref[:, span], tail_values, TN).astype(BF16)
    base = chip * 2 * TOK
    one, zero = jnp.float32(1), jnp.float32(0)

    def flag(condition):
        return jnp.where(condition, one, zero)

    def put(row, value):
        coef_ref[row : row + 1, :] = jnp.full((1, 128), value, F32)

    low = core == 0
    inner = flag(same(ends, base + 127, base + 255))
    across = flag(same(ends, base - 1, base + 127))
    put(CA, jnp.where(low, inner, one))
    put(CB, jnp.where(low, one, inner))
    put(MP, flag((chip >= 1) & same(ends, base - 1, base + 255)))
    put(ME1, flag(chip >= 1))
    put(ME3, flag((chip >= 3) & same(ends, base - 513, base - 1)))
    put(CS, jnp.where(low, one, zero))
    put(ES, jnp.where(low, across, one))
    put(CR, jnp.where(low, zero, one))
    put(ER, jnp.where(low, one, across))
    inner = flag(same(ends, base, base + 128))
    across = flag(same(ends, base + 128, base + 256))
    put(BACK + CA, jnp.where(low, one, inner))
    put(BACK + CB, jnp.where(low, inner, one))
    put(BACK + MP, flag((chip <= CHIPS - 2) & same(ends, base, base + 256)))
    put(BACK + ME1, flag(chip <= CHIPS - 2))
    put(BACK + ME3, flag((chip <= CHIPS - 4) & same(ends, base + 256, base + 768)))
    put(BACK + CS, jnp.where(low, zero, one))
    put(BACK + ES, jnp.where(low, one, across))
    put(BACK + CR, jnp.where(low, one, zero))
    put(BACK + ER, jnp.where(low, across, one))
    for row in range(2 * BACK, ROWS):
        put(row, zero)


def local_state(lengths, keys, values):
    half = jax.ShapeDtypeStruct((HALF, HEAD_DIM, HEAD_DIM), BF16)
    return pl.pallas_call(
        local_state_kernel,
        out_shape=(half, half, jax.ShapeDtypeStruct((ROWS, 128), F32)),
        in_specs=[SMEM, VMEM, VMEM],
        out_specs=(VMEM, VMEM, VMEM),
        compiler_params=params(),
        cost_estimate=cost(50_000_000, 1_200_000),
        name="local_state",
    )(lengths, keys, values)


def inside_kernel(lengths_ref, queries_ref, keys_ref, values_ref, attn_ref, inside_ref):
    chip, core = chip_and_core()
    ends = running_ends(lengths_ref)
    start = (chip * 2 + core) * TOK
    mask = same_doc_mask(ends, start)
    for h in range(HEADS):
        span = lanes(h)
        scores = dot(queries_ref[:, span], keys_ref[:, span], NT)
        attn = jnp.where(mask, scores, 0.0).astype(BF16)
        attn_ref[h] = attn
        inside_ref[:, span] = dot(attn, values_ref[:, span], NN)


def inside_part(lengths, queries, keys, values):
    return pl.pallas_call(
        inside_kernel,
        out_shape=(
            jax.ShapeDtypeStruct((HEADS, TOK, TOK), BF16),
            jax.ShapeDtypeStruct((TOK, DI), F32),
        ),
        in_specs=[SMEM, VMEM, VMEM, VMEM],
        out_specs=(VMEM, VMEM),
        compiler_params=params(),
        cost_estimate=cost(100_000_000, 2_400_000),
        name="inside_part",
    )(lengths, queries, keys, values)


def mixed_kernel(lengths_ref, queries_ref, inside_ref, mine_ref, other_ref, gain_ref, mixed_ref, scaled_ref):
    chip, core = chip_and_core()
    ends = running_ends(lengths_ref)
    start = (chip * 2 + core) * TOK
    carry = rows_of(start) < next_end(ends, start - 1)
    for part, ref in ((0, mine_ref), (1, other_ref)):
        first = HALF * core if part == 0 else HALF * (1 - core)
        for j in range(HALF):
            span = lanes(first + j)
            carried = dot(queries_ref[:, span], ref[j], NN)
            mixed = inside_ref[:, span] + jnp.where(carry, carried, 0.0)
            mixed_ref[:, span] = mixed
            inv_rms = lax.rsqrt(jnp.mean(mixed * mixed, axis=-1, keepdims=True) + EPSILON)
            scaled_ref[:, span] = (mixed * inv_rms * gain_ref[:, span]).astype(BF16)


def mixed_part(lengths, queries, inside, mine, other, gain):
    return pl.pallas_call(
        mixed_kernel,
        out_shape=(jax.ShapeDtypeStruct((TOK, DI), F32), jax.ShapeDtypeStruct((TOK, DI), BF16)),
        in_specs=[SMEM, VMEM, VMEM, VMEM, VMEM, VMEM],
        out_specs=(VMEM, VMEM),
        compiler_params=params(),
        cost_estimate=cost(50_000_000, 2_700_000),
        name="mixed_part",
    )(lengths, queries, inside, mine, other, gain)


PAIR = 2 * HEAD_DIM


def grad_mixed_kernel(
    core_ref, lengths_ref, cot_ref, weight_ref, mixed_ref, gain_ref, queries_ref, low_ref, give_ref, keep_ref
):
    step = pl.program_id(0)
    chip, core = chip_and_core()
    ends = running_ends(lengths_ref)
    start = (chip * 2 + core) * TOK
    head_rows = rows_of(start) < next_end(ends, start)
    grad_scaled = dot(cot_ref[:, : D // 2], weight_ref[0], NT) + dot(cot_ref[:, D // 2 :], weight_ref[1], NT)
    states = []
    for j in range(2):
        span = lanes(j)
        mixed = mixed_ref[:, span]
        inv_rms = lax.rsqrt(jnp.mean(mixed * mixed, axis=-1, keepdims=True) + EPSILON)
        normed = mixed * inv_rms
        g = grad_scaled[:, j * HEAD_DIM : (j + 1) * HEAD_DIM] * gain_ref[:, span]
        low = (inv_rms * (g - normed * jnp.mean(g * normed, axis=-1, keepdims=True))).astype(BF16)
        low_ref[:, span] = low
        head_queries = jnp.where(head_rows, queries_ref[:, span], 0)
        states.append(dot(head_queries, low, TN).astype(BF16))

    @pl.when(step < 3)
    def _():
        give_ref[0] = states[0]
        give_ref[1] = states[1]

    @pl.when(step >= 3)
    def _():
        keep_ref[0] = states[0]
        keep_ref[1] = states[1]


def grad_mixed_part(core_index, lengths, cotangent, weight, mixed, gain, queries):
    def pair(i, core_ref):
        return lax.rem(i + 3 * (1 - core_ref[0]), 6)

    half = jax.ShapeDtypeStruct((HALF, HEAD_DIM, HEAD_DIM), BF16)
    return pl.pallas_call(
        grad_mixed_kernel,
        out_shape=(jax.ShapeDtypeStruct((TOK, DI), BF16), half, half),
        grid_spec=pltpu.PrefetchScalarGridSpec(
            num_scalar_prefetch=1,
            grid=(6,),
            in_specs=[
                SMEM,
                pl.BlockSpec((TOK, D), lambda i, c: (0, 0)),
                pl.BlockSpec((2, PAIR, D // 2), lambda i, c: (0, pair(i, c), 0)),
                pl.BlockSpec((TOK, PAIR), lambda i, c: (0, pair(i, c))),
                pl.BlockSpec((1, PAIR), lambda i, c: (0, pair(i, c))),
                pl.BlockSpec((TOK, PAIR), lambda i, c: (0, pair(i, c))),
            ],
            out_specs=(
                pl.BlockSpec((TOK, PAIR), lambda i, c: (0, pair(i, c))),
                pl.BlockSpec((2, HEAD_DIM, HEAD_DIM), lambda i, c: (jnp.minimum(i, 2), 0, 0)),
                pl.BlockSpec((2, HEAD_DIM, HEAD_DIM), lambda i, c: (jnp.maximum(i - 3, 0), 0, 0)),
            ),
        ),
        compiler_params=params(58),
        cost_estimate=cost(860_000_000, 9_000_000),
        name="grad_mixed_part",
    )(core_index, lengths, cotangent, weight, mixed, gain, queries)


def output_kernel(scaled_ref, weight_ref, output_ref):
    output_ref[...] = dot(scaled_ref[...], weight_ref[0], NN).astype(BF16)


def output_part(scaled, weight):
    width = 512
    per = D // 2 // width
    return pl.pallas_call(
        output_kernel,
        out_shape=jax.ShapeDtypeStruct((TOK, D), BF16),
        grid=(D // width,),
        in_specs=[
            pl.BlockSpec((TOK, DI), lambda i: (0, 0)),
            pl.BlockSpec((1, DI, width), lambda i: (i // per, 0, i % per)),
        ],
        out_specs=pl.BlockSpec((TOK, width), lambda i: (0, i)),
        compiler_params=params(58),
        cost_estimate=cost(810_000_000, 7_500_000),
        name="output_part",
    )(scaled, weight)


def grads_kernel(
    lengths_ref, queries_ref, keys_ref, values_ref, low_ref, attn_ref, mine_ref, other_ref,
    dq_ref, dk_ref, dv_ref,
):
    chip, core = chip_and_core()
    ends = running_ends(lengths_ref)
    start = (chip * 2 + core) * TOK
    mask = same_doc_mask(ends, start)
    carry = rows_of(start) < next_end(ends, start - 1)
    for part, ref in ((0, mine_ref), (1, other_ref)):
        first = HALF * core if part == 0 else HALF * (1 - core)
        for j in range(HALF):
            span = lanes(first + j)
            low = low_ref[:, span]
            queries = queries_ref[:, span]
            grad_attn = jnp.where(mask, dot(low, values_ref[:, span], NT), 0.0).astype(BF16)
            from_state = jnp.where(carry, dot(low, ref[j], NT), 0.0)
            dq_ref[:, span] = (dot(grad_attn, keys_ref[:, span], NN) + from_state).astype(BF16)
            dk_ref[:, span] = dot(grad_attn, queries, TN)
            dv_ref[:, span] = dot(attn_ref[first + j], low, TN)


def grads_part(lengths, queries, keys, values, low, attn, mine, other):
    full = jax.ShapeDtypeStruct((TOK, DI), F32)
    return pl.pallas_call(
        grads_kernel,
        out_shape=(jax.ShapeDtypeStruct((TOK, DI), BF16), full, full),
        in_specs=[SMEM] + [VMEM] * 7,
        out_specs=(VMEM,) * 3,
        compiler_params=params(),
        cost_estimate=cost(250_000_000, 5_000_000),
        name="grads_part",
    )(lengths, queries, keys, values, low, attn, mine, other)


def last_kernel(lengths_ref, keys_ref, values_ref, dk_part_ref, dv_part_ref, mine_ref, other_ref, dk_ref, dv_ref):
    chip, core = chip_and_core()
    ends = running_ends(lengths_ref)
    start = (chip * 2 + core) * TOK
    after = rows_of(start) >= last_end(ends, start + TOK)
    for part, ref in ((0, mine_ref), (1, other_ref)):
        first = HALF * core if part == 0 else HALF * (1 - core)
        for j in range(HALF):
            span = lanes(first + j)
            state = ref[j]
            from_keys = jnp.where(after, dot(values_ref[:, span], state, NT), 0.0)
            dk_ref[:, span] = (dk_part_ref[:, span] + from_keys).astype(BF16)
            from_values = jnp.where(after, dot(keys_ref[:, span], state, NN), 0.0)
            dv_ref[:, span] = (dv_part_ref[:, span] + from_values).astype(BF16)


def last_part(lengths, keys, values, dk, dv, mine, other):
    full = jax.ShapeDtypeStruct((TOK, DI), BF16)
    return pl.pallas_call(
        last_kernel,
        out_shape=(full, full),
        in_specs=[SMEM] + [VMEM] * 6,
        out_specs=(VMEM,) * 2,
        compiler_params=params(),
        cost_estimate=cost(100_000_000, 3_500_000),
        name="last_part",
    )(lengths, keys, values, dk, dv, mine, other)


def swap_cores(block):
    return lax.ppermute(block, "core", [(0, 1), (1, 0)])


def from_chip(block, distance):
    chips = range(CHIPS)
    pairs = [(2 * (i - distance) + c, 2 * i + c) for i in chips for c in range(2) if i - distance in chips]
    return lax.ppermute(block, ("z", "x", "core"), pairs)


def window(keep, give, coef, sign):
    def row(index):
        return coef[index + (0 if sign > 0 else BACK)]

    got = swap_cores(give).astype(F32)
    own = keep.astype(F32)
    chip_sum = (row(CA) * own + row(CB) * got).astype(BF16)
    before = from_chip(chip_sum, sign)
    pair_sum = (chip_sum.astype(F32) + row(MP) * before.astype(F32)).astype(BF16)
    near = from_chip(pair_sum, sign)
    far = from_chip(pair_sum, 3 * sign)
    enter = row(ME1) * near.astype(F32) + row(ME3) * far.astype(F32)
    other = swap_cores((row(CS) * own + row(ES) * enter).astype(BF16))
    mine = (row(CR) * got + row(ER) * enter).astype(BF16)
    return mine, other


def layer(queries, keys, values, lengths, gain, out_weight, cotangent):
    queries, keys, values, cotangent = queries[0], keys[0], values[0], cotangent[0]
    core = lax.axis_index("core")
    part = lax.dynamic_slice(out_weight, (0, core * (D // 2)), (out_weight.shape[0], D // 2))
    gathered = lax.all_gather(part, ("core", "fsdp"), axis=0, tiled=True)
    weight = gathered.reshape(2, DI, D // 2)
    gain_row = gain.reshape(1, DI)
    core_index = jnp.full((1,), core, jnp.int32)

    keep, give, coef = local_state(lengths, keys, values)
    mine, other = window(keep, give, coef, 1)
    attn, inside = inside_part(lengths, queries, keys, values)
    mixed, scaled = mixed_part(lengths, queries, inside, mine, other, gain_row)
    low, give_back, keep_back = grad_mixed_part(core_index, lengths, cotangent, weight, mixed, gain_row, queries)
    back_mine, back_other = window(keep_back, give_back, coef, -1)
    output = output_part(scaled, weight)
    dq, dk_part, dv_part = grads_part(lengths, queries, keys, values, low, attn, mine, other)
    dk, dv = last_part(lengths, keys, values, dk_part, dv_part, back_mine, back_other)
    return output[None], dq[None], dk[None], dv[None]


def solution(mesh):
    split = Mesh(mesh.devices.reshape(8, 4, 2, 8), ("z", "x", "core", "fsdp"))
    tokens = P("fsdp", ("z", "x", "core"), None)
    return jax.shard_map(
        layer,
        mesh=split,
        in_specs=(tokens, tokens, tokens, P("fsdp", None), P(), P("fsdp", None), tokens),
        out_specs=(tokens,) * 4,
        check_vma=False,
    )
```

```python
import jax
import jax.numpy as jnp
from jax import lax
from jax.experimental import pallas as pl
from jax.experimental.pallas import tpu as pltpu
from jax.sharding import Mesh, PartitionSpec as P


HEADS = 12
HALF = 6
HEAD_DIM = 128
NDOCS = 16
TOK = 128
SHARD = 192
Y = 8
DI = HEADS * HEAD_DIM
D = 2048
CHIPS = 32
EPSILON = 1.0
F32 = jnp.float32
BF16 = jnp.bfloat16

CA, CB, MP, ME1, ME3, CS, ES, CR, ER = range(9)
BACK = 9
ROWS = 24

VMEM = pl.BlockSpec(memory_space=pltpu.VMEM)
SMEM = pl.BlockSpec(memory_space=pltpu.SMEM)
HBM = pl.BlockSpec(memory_space=pltpu.HBM)


def params(mib=24):
    return pltpu.CompilerParams(vmem_limit_bytes=mib << 20)


def cost(flops, moved):
    return pl.CostEstimate(flops=flops, bytes_accessed=moved, transcendentals=0)


def chip_and_core():
    return lax.axis_index("z") * 4 + lax.axis_index("x"), lax.axis_index("core")


def running_ends(lengths_ref):
    ends, total = [], jnp.int32(0)
    for j in range(NDOCS):
        total = total + lengths_ref[0, j]
        ends.append(total)
    return ends


def last_end(ends, position):
    best = jnp.int32(-(1 << 30))
    for end in ends:
        best = jnp.where(end <= position, end, best)
    return best


def next_end(ends, position):
    best = jnp.int32(1 << 30)
    for end in reversed(ends):
        best = jnp.where(end > position, end, best)
    return best


def same(ends, early, late):
    return last_end(ends, late) <= early


def lanes(head):
    start = head * HEAD_DIM
    return pl.ds(start if isinstance(head, int) else pl.multiple_of(start, HEAD_DIM), HEAD_DIM)


def dot(a, b, contract):
    return lax.dot_general(a, b, ((contract[0], contract[1]), ((), ())), preferred_element_type=F32)


NN = ((1,), (0,))
NT = ((1,), (1,))
TN = ((0,), (0,))


def rows_of(start, width=HEAD_DIM):
    return start + lax.broadcasted_iota(jnp.int32, (TOK, width), 0)


def same_doc_mask(ends, start):
    rows = rows_of(start)
    columns = start + lax.broadcasted_iota(jnp.int32, (TOK, TOK), 1)
    first = jnp.full((TOK, TOK), -(1 << 30), jnp.int32)
    for end in ends:
        first = jnp.where(end <= rows, end, first)
    return (columns <= rows) & (columns >= first)


def take_half_kernel(weight_ref, cot_ref, half_ref, cot_keep_ref, cot_give_ref, sems):
    _, core = chip_and_core()
    width = D // 2
    mine = pl.ds(pl.multiple_of(core * width, width), width)
    theirs = pl.ds(pl.multiple_of((1 - core) * width, width), width)
    copies = [
        pltpu.make_async_copy(weight_ref.at[:, mine], half_ref, sems.at[0]),
        pltpu.make_async_copy(cot_ref.at[:, theirs], cot_give_ref, sems.at[1]),
        pltpu.make_async_copy(cot_ref.at[:, mine], cot_keep_ref, sems.at[2]),
    ]
    for copy in copies:
        copy.start()
    for copy in copies:
        copy.wait()


def take_half(weight, cotangent):
    cot = jax.ShapeDtypeStruct((TOK, D // 2), BF16)
    return pl.pallas_call(
        take_half_kernel,
        out_shape=(jax.ShapeDtypeStruct((SHARD, D // 2), BF16), cot, cot),
        in_specs=[HBM, HBM],
        out_specs=(VMEM, VMEM, VMEM),
        scratch_shapes=[pltpu.SemaphoreType.DMA((3,))],
        compiler_params=params(60),
        cost_estimate=cost(1000, 2_000_000),
        name="take_half",
    )(weight, cotangent)


def local_state_kernel(
    lengths_ref, keys_hbm, values_hbm, keep_ref, give_ref, coef_ref, keys_ref, values_ref, sems
):
    copies = [
        pltpu.make_async_copy(keys_hbm, keys_ref, sems.at[0]),
        pltpu.make_async_copy(values_hbm, values_ref, sems.at[1]),
    ]
    for copy in copies:
        copy.start()
    for copy in copies:
        copy.wait()
    chip, core = chip_and_core()
    ends = running_ends(lengths_ref)
    start = (chip * 2 + core) * TOK
    tail = rows_of(start) >= last_end(ends, start + TOK - 1)
    for part, ref in ((0, keep_ref), (1, give_ref)):
        first = HALF * core if part == 0 else HALF * (1 - core)
        for j in range(HALF):
            span = lanes(first + j)
            tail_values = jnp.where(tail, values_ref[:, span], 0)
            ref[j] = dot(keys_ref[:, span], tail_values, TN).astype(BF16)
    base = chip * 2 * TOK
    one, zero = jnp.float32(1), jnp.float32(0)

    def flag(condition):
        return jnp.where(condition, one, zero)

    def put(row, value):
        coef_ref[row : row + 1, :] = jnp.full((1, 128), value, F32)

    low = core == 0
    inner = flag(same(ends, base + 127, base + 255))
    across = flag(same(ends, base - 1, base + 127))
    put(CA, jnp.where(low, inner, one))
    put(CB, jnp.where(low, one, inner))
    put(MP, flag((chip >= 1) & same(ends, base - 1, base + 255)))
    put(ME1, flag(chip >= 1))
    put(ME3, flag((chip >= 3) & same(ends, base - 513, base - 1)))
    put(CS, jnp.where(low, one, zero))
    put(ES, jnp.where(low, across, one))
    put(CR, jnp.where(low, zero, one))
    put(ER, jnp.where(low, one, across))
    inner = flag(same(ends, base, base + 128))
    across = flag(same(ends, base + 128, base + 256))
    put(BACK + CA, jnp.where(low, one, inner))
    put(BACK + CB, jnp.where(low, inner, one))
    put(BACK + MP, flag((chip <= CHIPS - 2) & same(ends, base, base + 256)))
    put(BACK + ME1, flag(chip <= CHIPS - 2))
    put(BACK + ME3, flag((chip <= CHIPS - 4) & same(ends, base + 256, base + 768)))
    put(BACK + CS, jnp.where(low, zero, one))
    put(BACK + ES, jnp.where(low, one, across))
    put(BACK + CR, jnp.where(low, one, zero))
    put(BACK + ER, jnp.where(low, across, one))
    for row in range(2 * BACK, ROWS):
        put(row, zero)


def local_state(lengths, keys, values):
    half = jax.ShapeDtypeStruct((HALF, HEAD_DIM, HEAD_DIM), BF16)
    return pl.pallas_call(
        local_state_kernel,
        out_shape=(half, half, jax.ShapeDtypeStruct((ROWS, 128), F32)),
        in_specs=[SMEM, HBM, HBM],
        out_specs=(VMEM, VMEM, VMEM),
        scratch_shapes=[
            pltpu.VMEM((TOK, DI), BF16),
            pltpu.VMEM((TOK, DI), BF16),
            pltpu.SemaphoreType.DMA((2,)),
        ],
        compiler_params=params(),
        cost_estimate=cost(50_000_000, 1_200_000),
        name="local_state",
    )(lengths, keys, values)


def inside_kernel(lengths_ref, queries_ref, keys_ref, values_ref, attn_ref, inside_ref):
    chip, core = chip_and_core()
    ends = running_ends(lengths_ref)
    start = (chip * 2 + core) * TOK
    mask = same_doc_mask(ends, start)
    for h in range(HEADS):
        span = lanes(h)
        scores = dot(queries_ref[:, span], keys_ref[:, span], NT)
        attn = jnp.where(mask, scores, 0.0).astype(BF16)
        attn_ref[h] = attn
        inside_ref[:, span] = dot(attn, values_ref[:, span], NN)


def inside_part(lengths, queries, keys, values):
    return pl.pallas_call(
        inside_kernel,
        out_shape=(
            jax.ShapeDtypeStruct((HEADS, TOK, TOK), BF16),
            jax.ShapeDtypeStruct((TOK, DI), F32),
        ),
        in_specs=[SMEM, VMEM, VMEM, VMEM],
        out_specs=(VMEM, VMEM),
        compiler_params=params(),
        cost_estimate=cost(100_000_000, 2_400_000),
        name="inside_part",
    )(lengths, queries, keys, values)


def mixed_kernel(lengths_ref, queries_ref, inside_ref, mine_ref, other_ref, gain_ref, mixed_ref, scaled_ref):
    chip, core = chip_and_core()
    ends = running_ends(lengths_ref)
    start = (chip * 2 + core) * TOK
    carry = rows_of(start) < next_end(ends, start - 1)
    for part, ref in ((0, mine_ref), (1, other_ref)):
        first = HALF * core if part == 0 else HALF * (1 - core)
        for j in range(HALF):
            span = lanes(first + j)
            carried = dot(queries_ref[:, span], ref[j], NN)
            mixed = inside_ref[:, span] + jnp.where(carry, carried, 0.0)
            mixed_ref[:, span] = mixed
            inv_rms = lax.rsqrt(jnp.mean(mixed * mixed, axis=-1, keepdims=True) + EPSILON)
            scaled_ref[:, span] = (mixed * inv_rms * gain_ref[:, span]).astype(BF16)


def mixed_part(lengths, queries, inside, mine, other, gain):
    return pl.pallas_call(
        mixed_kernel,
        out_shape=(jax.ShapeDtypeStruct((TOK, DI), F32), jax.ShapeDtypeStruct((TOK, DI), BF16)),
        in_specs=[SMEM, VMEM, VMEM, VMEM, VMEM, VMEM],
        out_specs=(VMEM, VMEM),
        compiler_params=params(),
        cost_estimate=cost(50_000_000, 2_700_000),
        name="mixed_part",
    )(lengths, queries, inside, mine, other, gain)


def shard_rows(distance, count=SHARD, skip=0):
    owner = lax.rem(lax.axis_index("fsdp") + (distance + Y), Y)
    return pl.ds(pl.multiple_of(owner * SHARD + skip, 32), count)


EARLY = (0, -1, 1, -2, 2, -3, 3)


def share_kernel(cot_keep_ref, cot_got_ref, *refs):
    pieces, (own_ref, give_ref, cot_ref) = refs[: len(EARLY)], refs[len(EARLY) :]
    cot_ref[:TOK] = cot_keep_ref[...]
    cot_ref[TOK:] = cot_got_ref[...]
    for distance, piece in zip(EARLY, pieces):
        share = dot(piece[...], cot_ref[...], NT)
        rows = shard_rows(distance)
        own_ref[rows, :] = share[:, :TOK]
        give_ref[rows, :] = share[:, TOK:].astype(BF16)


SHARE_SHAPES = (jax.ShapeDtypeStruct((DI, TOK), F32), jax.ShapeDtypeStruct((DI, TOK), BF16))


def share_part(cot_keep, cot_got, pieces):
    return pl.pallas_call(
        share_kernel,
        out_shape=SHARE_SHAPES,
        in_specs=[VMEM] * (2 + len(EARLY)),
        out_specs=(VMEM, VMEM),
        scratch_shapes=[pltpu.VMEM((2 * TOK, D // 2), BF16)],
        compiler_params=params(),
        cost_estimate=cost(700_000_000, 4_500_000),
        name="share_part",
    )(cot_keep, cot_got, *pieces)


def share_end_kernel(
    cot_keep_ref, cot_got_ref, top_ref, bottom_ref, own_in_ref, give_in_ref, own_ref, give_ref, cot_ref, piece_ref
):
    cot_ref[:TOK] = cot_keep_ref[...]
    cot_ref[TOK:] = cot_got_ref[...]
    piece_ref[: SHARD // 2] = top_ref[...]
    piece_ref[SHARD // 2 :] = bottom_ref[...]
    own_ref[...] = own_in_ref[...]
    give_ref[...] = give_in_ref[...]
    share = dot(piece_ref[...], cot_ref[...], NT)
    rows = shard_rows(4)
    own_ref[rows, :] = share[:, :TOK]
    give_ref[rows, :] = share[:, TOK:].astype(BF16)


def share_end(cot_keep, cot_got, top, bottom, own, give):
    return pl.pallas_call(
        share_end_kernel,
        out_shape=SHARE_SHAPES,
        in_specs=[VMEM] * 6,
        out_specs=(VMEM, VMEM),
        scratch_shapes=[pltpu.VMEM((2 * TOK, D // 2), BF16), pltpu.VMEM((SHARD, D // 2), BF16)],
        compiler_params=params(),
        cost_estimate=cost(100_000_000, 3_500_000),
        name="share_end",
    )(cot_keep, cot_got, top, bottom, own, give)


def grad_mixed_kernel(
    lengths_ref, own_ref, got_ref, mixed_ref, gain_ref, queries_ref, low_ref, give_ref, keep_ref
):
    chip, core = chip_and_core()
    ends = running_ends(lengths_ref)
    start = (chip * 2 + core) * TOK
    head_rows = rows_of(start) < next_end(ends, start)
    for part, ref in ((0, give_ref), (1, keep_ref)):
        first = HALF * (1 - core) if part == 0 else HALF * core
        for j in range(HALF):
            span = lanes(first + j)
            grad_scaled = (own_ref[span, :] + got_ref[span, :].astype(F32)).T
            mixed = mixed_ref[:, span]
            inv_rms = lax.rsqrt(jnp.mean(mixed * mixed, axis=-1, keepdims=True) + EPSILON)
            normed = mixed * inv_rms
            g = grad_scaled * gain_ref[:, span]
            low = (inv_rms * (g - normed * jnp.mean(g * normed, axis=-1, keepdims=True))).astype(BF16)
            low_ref[:, span] = low
            head_queries = jnp.where(head_rows, queries_ref[:, span], 0)
            ref[j] = dot(head_queries, low, TN).astype(BF16)


def grad_mixed_part(lengths, own, got, mixed, gain, queries):
    half = jax.ShapeDtypeStruct((HALF, HEAD_DIM, HEAD_DIM), BF16)
    return pl.pallas_call(
        grad_mixed_kernel,
        out_shape=(jax.ShapeDtypeStruct((TOK, DI), BF16), half, half),
        in_specs=[SMEM] + [VMEM] * 5,
        out_specs=(VMEM,) * 3,
        compiler_params=params(),
        cost_estimate=cost(60_000_000, 4_000_000),
        name="grad_mixed_part",
    )(lengths, own, got, mixed, gain, queries)


def output_kernel(scaled_ref, scaled_got_ref, *refs):
    pieces, (top_ref, bottom_ref, own_ref, give_ref, both_ref, weight_ref) = refs[: len(EARLY)], refs[len(EARLY) :]
    for distance, piece in zip(EARLY, pieces):
        weight_ref[shard_rows(distance), :] = piece[...]
    weight_ref[shard_rows(4, SHARD // 2), :] = top_ref[...]
    weight_ref[shard_rows(4, SHARD // 2, SHARD // 2), :] = bottom_ref[...]
    both_ref[:TOK] = scaled_ref[...]
    both_ref[TOK:] = scaled_got_ref[...]
    for start in range(0, D // 2, 256):
        block = dot(both_ref[...], weight_ref[:, start : start + 256], NN).astype(BF16)
        own_ref[:, start : start + 256] = block[:TOK]
        give_ref[:, start : start + 256] = block[TOK:]


def output_part(scaled, scaled_got, pieces, top, bottom):
    half = jax.ShapeDtypeStruct((TOK, D // 2), BF16)
    return pl.pallas_call(
        output_kernel,
        out_shape=(half, half),
        in_specs=[VMEM] * (4 + len(EARLY)),
        out_specs=(VMEM, VMEM),
        scratch_shapes=[pltpu.VMEM((2 * TOK, DI), BF16), pltpu.VMEM((DI, D // 2), BF16)],
        compiler_params=params(),
        cost_estimate=cost(810_000_000, 5_000_000),
        name="output_part",
    )(scaled, scaled_got, *pieces, top, bottom)


def grads_kernel(
    lengths_ref, queries_ref, keys_ref, values_ref, low_ref, attn_ref, mine_ref, other_ref,
    dq_ref, dk_ref, dv_ref,
):
    chip, core = chip_and_core()
    ends = running_ends(lengths_ref)
    start = (chip * 2 + core) * TOK
    mask = same_doc_mask(ends, start)
    carry = rows_of(start) < next_end(ends, start - 1)
    for part, ref in ((0, mine_ref), (1, other_ref)):
        first = HALF * core if part == 0 else HALF * (1 - core)
        for j in range(HALF):
            span = lanes(first + j)
            low = low_ref[:, span]
            queries = queries_ref[:, span]
            grad_attn = jnp.where(mask, dot(low, values_ref[:, span], NT), 0.0).astype(BF16)
            from_state = jnp.where(carry, dot(low, ref[j], NT), 0.0)
            dq_ref[:, span] = (dot(grad_attn, keys_ref[:, span], NN) + from_state).astype(BF16)
            dk_ref[:, span] = dot(grad_attn, queries, TN)
            dv_ref[:, span] = dot(attn_ref[first + j], low, TN)


def grads_part(lengths, queries, keys, values, low, attn, mine, other):
    full = jax.ShapeDtypeStruct((TOK, DI), F32)
    return pl.pallas_call(
        grads_kernel,
        out_shape=(jax.ShapeDtypeStruct((TOK, DI), BF16), full, full),
        in_specs=[SMEM] + [VMEM] * 7,
        out_specs=(VMEM,) * 3,
        compiler_params=params(),
        cost_estimate=cost(250_000_000, 5_000_000),
        name="grads_part",
    )(lengths, queries, keys, values, low, attn, mine, other)


def last_kernel(
    lengths_ref, keys_ref, values_ref, dk_part_ref, dv_part_ref, out_own_ref, out_got_ref, mine_ref, other_ref,
    dk_ref, dv_ref, output_ref,
):
    chip, core = chip_and_core()
    width = D // 2
    output_ref[:, pl.ds(pl.multiple_of(core * width, width), width)] = out_own_ref[...]
    output_ref[:, pl.ds(pl.multiple_of((1 - core) * width, width), width)] = out_got_ref[...]
    ends = running_ends(lengths_ref)
    start = (chip * 2 + core) * TOK
    after = rows_of(start) >= last_end(ends, start + TOK)
    for part, ref in ((0, mine_ref), (1, other_ref)):
        first = HALF * core if part == 0 else HALF * (1 - core)
        for j in range(HALF):
            span = lanes(first + j)
            state = ref[j]
            from_keys = jnp.where(after, dot(values_ref[:, span], state, NT), 0.0)
            dk_ref[:, span] = (dk_part_ref[:, span] + from_keys).astype(BF16)
            from_values = jnp.where(after, dot(keys_ref[:, span], state, NN), 0.0)
            dv_ref[:, span] = (dv_part_ref[:, span] + from_values).astype(BF16)


def last_part(lengths, keys, values, dk, dv, out_own, out_got, mine, other):
    full = jax.ShapeDtypeStruct((TOK, DI), BF16)
    return pl.pallas_call(
        last_kernel,
        out_shape=(full, full, jax.ShapeDtypeStruct((TOK, D), BF16)),
        in_specs=[SMEM] + [VMEM] * 8,
        out_specs=(VMEM,) * 3,
        compiler_params=params(),
        cost_estimate=cost(100_000_000, 4_500_000),
        name="last_part",
    )(lengths, keys, values, dk, dv, out_own, out_got, mine, other)


def swap_cores(block):
    return lax.ppermute(block, "core", [(0, 1), (1, 0)])


def from_chip(block, distance):
    chips = range(CHIPS)
    pairs = [(2 * (i - distance) + c, 2 * i + c) for i in chips for c in range(2) if i - distance in chips]
    return lax.ppermute(block, ("z", "x", "core"), pairs)


def along_y(block, distance):
    return lax.ppermute(block, "fsdp", [(i, (i + distance) % Y) for i in range(Y)])


def window(keep, give, coef, sign):
    def row(index):
        return coef[index + (0 if sign > 0 else BACK)]

    got = swap_cores(give).astype(F32)
    own = keep.astype(F32)
    chip_sum = (row(CA) * own + row(CB) * got).astype(BF16)
    before = from_chip(chip_sum, sign)
    pair_sum = (chip_sum.astype(F32) + row(MP) * before.astype(F32)).astype(BF16)
    near = from_chip(pair_sum, sign)
    far = from_chip(pair_sum, 3 * sign)
    enter = row(ME1) * near.astype(F32) + row(ME3) * far.astype(F32)
    other = swap_cores((row(CS) * own + row(ES) * enter).astype(BF16))
    mine = (row(CR) * got + row(ER) * enter).astype(BF16)
    return mine, other


def layer(queries, keys, values, lengths, gain, out_weight, cotangent):
    queries, keys, values, cotangent = queries[0], keys[0], values[0], cotangent[0]
    gain_row = gain.reshape(1, DI)
    half, cot_keep, cot_give = take_half(out_weight, cotangent)
    up, down = [half], [half]
    for _ in range(1, 4):
        up.append(along_y(up[-1], 1))
        down.append(along_y(down[-1], -1))
    top = along_y(up[3][: SHARD // 2], 1)
    bottom = along_y(down[3][SHARD // 2 :], -1)
    pieces = (half, up[1], down[1], up[2], down[2], up[3], down[3])
    cot_got = swap_cores(cot_give)

    keep, give, coef = local_state(lengths, keys, values)
    mine, other = window(keep, give, coef, 1)
    attn, inside = inside_part(lengths, queries, keys, values)
    mixed, scaled = mixed_part(lengths, queries, inside, mine, other, gain_row)
    scaled_got = swap_cores(scaled)
    own_share, give_share = share_part(cot_keep, cot_got, pieces)
    own_share, give_share = share_end(cot_keep, cot_got, top, bottom, own_share, give_share)
    got_share = swap_cores(give_share)
    low, give_back, keep_back = grad_mixed_part(lengths, own_share, got_share, mixed, gain_row, queries)
    back_mine, back_other = window(keep_back, give_back, coef, -1)
    out_own, out_give = output_part(scaled, scaled_got, pieces, top, bottom)
    out_got = swap_cores(out_give)
    dq, dk_part, dv_part = grads_part(lengths, queries, keys, values, low, attn, mine, other)
    dk, dv, output = last_part(lengths, keys, values, dk_part, dv_part, out_own, out_got, back_mine, back_other)
    return output[None], dq[None], dk[None], dv[None]


def solution(mesh):
    split = Mesh(mesh.devices.reshape(8, 4, 2, 8), ("z", "x", "core", "fsdp"))
    tokens = P("fsdp", ("z", "x", "core"), None)
    return jax.shard_map(
        layer,
        mesh=split,
        in_specs=(tokens, tokens, tokens, P("fsdp", None), P(), P("fsdp", None), tokens),
        out_specs=(tokens,) * 4,
        check_vma=False,
    )
```

```python
import jax
import jax.numpy as jnp
from jax import lax
from jax.experimental import pallas as pl
from jax.experimental.pallas import tpu as pltpu
from jax.sharding import Mesh, PartitionSpec as P


HEADS = 12
HALF = 6
HEAD_DIM = 128
NDOCS = 16
TOK = 128
SHARD = 192
Y = 8
DI = HEADS * HEAD_DIM
D = 2048
CHIPS = 32
EPSILON = 1.0
F32 = jnp.float32
BF16 = jnp.bfloat16

CA, CB, MP, ME1, ME3, CS, ES, CR, ER = range(9)
BACK = 9
BACK_2, BACK_4 = 18, 19
ROWS = 24

VMEM = pl.BlockSpec(memory_space=pltpu.VMEM)
SMEM = pl.BlockSpec(memory_space=pltpu.SMEM)
HBM = pl.BlockSpec(memory_space=pltpu.HBM)


def params(mib=24):
    return pltpu.CompilerParams(vmem_limit_bytes=mib << 20)


def cost(flops, moved):
    return pl.CostEstimate(flops=flops, bytes_accessed=moved, transcendentals=0)


def chip_and_core():
    return lax.axis_index("z") * 4 + lax.axis_index("x"), lax.axis_index("core")


def running_ends(lengths_ref):
    ends, total = [], jnp.int32(0)
    for j in range(NDOCS):
        total = total + lengths_ref[0, j]
        ends.append(total)
    return ends


def last_end(ends, position):
    best = jnp.int32(-(1 << 30))
    for end in ends:
        best = jnp.where(end <= position, end, best)
    return best


def next_end(ends, position):
    best = jnp.int32(1 << 30)
    for end in reversed(ends):
        best = jnp.where(end > position, end, best)
    return best


def same(ends, early, late):
    return last_end(ends, late) <= early


def lanes(head):
    start = head * HEAD_DIM
    return pl.ds(start if isinstance(head, int) else pl.multiple_of(start, HEAD_DIM), HEAD_DIM)


def dot(a, b, contract):
    return lax.dot_general(a, b, ((contract[0], contract[1]), ((), ())), preferred_element_type=F32)


NN = ((1,), (0,))
NT = ((1,), (1,))
TN = ((0,), (0,))


def rows_of(start, width=HEAD_DIM):
    return start + lax.broadcasted_iota(jnp.int32, (TOK, width), 0)


def same_doc_mask(ends, start):
    rows = rows_of(start)
    columns = start + lax.broadcasted_iota(jnp.int32, (TOK, TOK), 1)
    first = jnp.full((TOK, TOK), -(1 << 30), jnp.int32)
    for end in ends:
        first = jnp.where(end <= rows, end, first)
    return (columns <= rows) & (columns >= first)


def take_half_kernel(weight_ref, cot_ref, half_ref, cot_keep_ref, cot_give_ref, sems):
    _, core = chip_and_core()
    width = D // 2
    mine = pl.ds(pl.multiple_of(core * width, width), width)
    theirs = pl.ds(pl.multiple_of((1 - core) * width, width), width)
    copies = [
        pltpu.make_async_copy(weight_ref.at[:, mine], half_ref, sems.at[0]),
        pltpu.make_async_copy(cot_ref.at[:, theirs], cot_give_ref, sems.at[1]),
        pltpu.make_async_copy(cot_ref.at[:, mine], cot_keep_ref, sems.at[2]),
    ]
    for copy in copies:
        copy.start()
    for copy in copies:
        copy.wait()


def take_half(weight, cotangent):
    cot = jax.ShapeDtypeStruct((TOK, D // 2), BF16)
    return pl.pallas_call(
        take_half_kernel,
        out_shape=(jax.ShapeDtypeStruct((SHARD, D // 2), BF16), cot, cot),
        in_specs=[HBM, HBM],
        out_specs=(VMEM, VMEM, VMEM),
        scratch_shapes=[pltpu.SemaphoreType.DMA((3,))],
        compiler_params=params(60),
        cost_estimate=cost(1000, 2_000_000),
        name="take_half",
    )(weight, cotangent)


def local_state_kernel(
    lengths_ref, keys_hbm, values_hbm, keep_ref, give_ref, coef_ref, keys_ref, values_ref, sems
):
    copies = [
        pltpu.make_async_copy(keys_hbm, keys_ref, sems.at[0]),
        pltpu.make_async_copy(values_hbm, values_ref, sems.at[1]),
    ]
    for copy in copies:
        copy.start()
    for copy in copies:
        copy.wait()
    chip, core = chip_and_core()
    ends = running_ends(lengths_ref)
    start = (chip * 2 + core) * TOK
    tail = rows_of(start) >= last_end(ends, start + TOK - 1)
    for part, ref in ((0, keep_ref), (1, give_ref)):
        first = HALF * core if part == 0 else HALF * (1 - core)
        for j in range(HALF):
            span = lanes(first + j)
            tail_values = jnp.where(tail, values_ref[:, span], 0)
            ref[j] = dot(keys_ref[:, span], tail_values, TN).astype(BF16)
    base = chip * 2 * TOK
    one, zero = jnp.float32(1), jnp.float32(0)

    def flag(condition):
        return jnp.where(condition, one, zero)

    def put(row, value):
        coef_ref[row : row + 1, :] = jnp.full((1, 128), value, F32)

    low = core == 0
    inner = flag(same(ends, base + 127, base + 255))
    across = flag(same(ends, base - 1, base + 127))
    put(CA, jnp.where(low, inner, one))
    put(CB, jnp.where(low, one, inner))
    put(MP, flag((chip >= 1) & same(ends, base - 1, base + 255)))
    put(ME1, flag(chip >= 1))
    put(ME3, flag((chip >= 3) & same(ends, base - 513, base - 1)))
    put(CS, jnp.where(low, one, zero))
    put(ES, jnp.where(low, across, one))
    put(CR, jnp.where(low, zero, one))
    put(ER, jnp.where(low, one, across))
    inner = flag(same(ends, base, base + 128))
    across = flag(same(ends, base + 128, base + 256))
    put(BACK + CA, jnp.where(low, one, inner))
    put(BACK + CB, jnp.where(low, inner, one))
    put(BACK + MP, flag((chip <= CHIPS - 2) & same(ends, base, base + 256)))
    put(BACK + ME1, flag(chip <= CHIPS - 2))
    put(BACK + ME3, flag((chip <= CHIPS - 4) & same(ends, base + 256, base + 768)))
    put(BACK + CS, jnp.where(low, zero, one))
    put(BACK + ES, jnp.where(low, one, across))
    put(BACK + CR, jnp.where(low, one, zero))
    put(BACK + ER, jnp.where(low, across, one))
    put(BACK_2, flag((chip <= CHIPS - 3) & same(ends, base + 256, base + 512)))
    put(BACK_4, flag((chip <= CHIPS - 5) & same(ends, base + 256, base + 1024)))
    for row in range(BACK_4 + 1, ROWS):
        put(row, zero)


def local_state(lengths, keys, values):
    half = jax.ShapeDtypeStruct((HALF, HEAD_DIM, HEAD_DIM), BF16)
    return pl.pallas_call(
        local_state_kernel,
        out_shape=(half, half, jax.ShapeDtypeStruct((ROWS, 128), F32)),
        in_specs=[SMEM, HBM, HBM],
        out_specs=(VMEM, VMEM, VMEM),
        scratch_shapes=[
            pltpu.VMEM((TOK, DI), BF16),
            pltpu.VMEM((TOK, DI), BF16),
            pltpu.SemaphoreType.DMA((2,)),
        ],
        compiler_params=params(),
        cost_estimate=cost(50_000_000, 1_200_000),
        name="local_state",
    )(lengths, keys, values)


def inside_kernel(lengths_ref, queries_ref, keys_ref, values_ref, attn_ref, inside_ref):
    chip, core = chip_and_core()
    ends = running_ends(lengths_ref)
    start = (chip * 2 + core) * TOK
    mask = same_doc_mask(ends, start)
    for h in range(HEADS):
        span = lanes(h)
        scores = dot(queries_ref[:, span], keys_ref[:, span], NT)
        attn = jnp.where(mask, scores, 0.0).astype(BF16)
        attn_ref[h] = attn
        inside_ref[:, span] = dot(attn, values_ref[:, span], NN)


def inside_part(lengths, queries, keys, values):
    return pl.pallas_call(
        inside_kernel,
        out_shape=(
            jax.ShapeDtypeStruct((HEADS, TOK, TOK), BF16),
            jax.ShapeDtypeStruct((TOK, DI), F32),
        ),
        in_specs=[SMEM, VMEM, VMEM, VMEM],
        out_specs=(VMEM, VMEM),
        compiler_params=params(),
        cost_estimate=cost(100_000_000, 2_400_000),
        name="inside_part",
    )(lengths, queries, keys, values)


def mixed_kernel(lengths_ref, queries_ref, inside_ref, mine_ref, other_ref, gain_ref, mixed_ref, scaled_ref):
    chip, core = chip_and_core()
    ends = running_ends(lengths_ref)
    start = (chip * 2 + core) * TOK
    carry = rows_of(start) < next_end(ends, start - 1)
    for part, ref in ((0, mine_ref), (1, other_ref)):
        first = HALF * core if part == 0 else HALF * (1 - core)
        for j in range(HALF):
            span = lanes(first + j)
            carried = dot(queries_ref[:, span], ref[j], NN)
            mixed = inside_ref[:, span] + jnp.where(carry, carried, 0.0)
            mixed_ref[:, span] = mixed
            inv_rms = lax.rsqrt(jnp.mean(mixed * mixed, axis=-1, keepdims=True) + EPSILON)
            scaled_ref[:, span] = (mixed * inv_rms * gain_ref[:, span]).astype(BF16)


def mixed_part(lengths, queries, inside, mine, other, gain):
    return pl.pallas_call(
        mixed_kernel,
        out_shape=(jax.ShapeDtypeStruct((TOK, DI), F32), jax.ShapeDtypeStruct((TOK, DI), BF16)),
        in_specs=[SMEM, VMEM, VMEM, VMEM, VMEM, VMEM],
        out_specs=(VMEM, VMEM),
        compiler_params=params(),
        cost_estimate=cost(50_000_000, 2_700_000),
        name="mixed_part",
    )(lengths, queries, inside, mine, other, gain)


def shard_rows(step):
    way = 2 * lax.axis_index("core") - 1
    owner = lax.rem(lax.axis_index("fsdp") + Y + way * step, Y)
    return pl.ds(pl.multiple_of(owner * SHARD, 64), SHARD)


EARLY = range(Y - 1)


def share_kernel(cot_keep_ref, cot_got_ref, *refs):
    pieces, (own_ref, give_ref, cot_ref) = refs[: len(EARLY)], refs[len(EARLY) :]
    cot_ref[:TOK] = cot_keep_ref[...]
    cot_ref[TOK:] = cot_got_ref[...]
    for step, piece in zip(EARLY, pieces):
        share = dot(piece[...], cot_ref[...], NT)
        rows = shard_rows(step)
        own_ref[rows, :] = share[:, :TOK]
        give_ref[rows, :] = share[:, TOK:].astype(BF16)


SHARE_SHAPES = (jax.ShapeDtypeStruct((DI, TOK), F32), jax.ShapeDtypeStruct((DI, TOK), BF16))


def share_part(cot_keep, cot_got, pieces):
    return pl.pallas_call(
        share_kernel,
        out_shape=SHARE_SHAPES,
        in_specs=[VMEM] * (2 + len(EARLY)),
        out_specs=(VMEM, VMEM),
        scratch_shapes=[pltpu.VMEM((2 * TOK, D // 2), BF16)],
        compiler_params=params(),
        cost_estimate=cost(700_000_000, 4_500_000),
        name="share_part",
    )(cot_keep, cot_got, *pieces)


def share_end_kernel(
    cot_keep_ref, cot_got_ref, piece_ref, own_in_ref, give_in_ref, own_ref, give_ref, cot_ref
):
    cot_ref[:TOK] = cot_keep_ref[...]
    cot_ref[TOK:] = cot_got_ref[...]
    own_ref[...] = own_in_ref[...]
    give_ref[...] = give_in_ref[...]
    share = dot(piece_ref[...], cot_ref[...], NT)
    rows = shard_rows(Y - 1)
    own_ref[rows, :] = share[:, :TOK]
    give_ref[rows, :] = share[:, TOK:].astype(BF16)


def share_end(cot_keep, cot_got, piece, own, give):
    return pl.pallas_call(
        share_end_kernel,
        out_shape=SHARE_SHAPES,
        in_specs=[VMEM] * 5,
        out_specs=(VMEM, VMEM),
        scratch_shapes=[pltpu.VMEM((2 * TOK, D // 2), BF16)],
        compiler_params=params(),
        cost_estimate=cost(100_000_000, 3_500_000),
        name="share_end",
    )(cot_keep, cot_got, piece, own, give)


def grad_mixed_kernel(
    lengths_ref, own_ref, got_ref, mixed_ref, gain_ref, queries_ref, low_ref, give_ref, keep_ref
):
    chip, core = chip_and_core()
    ends = running_ends(lengths_ref)
    start = (chip * 2 + core) * TOK
    head_rows = rows_of(start) < next_end(ends, start)
    for part, ref in ((0, give_ref), (1, keep_ref)):
        first = HALF * (1 - core) if part == 0 else HALF * core
        for j in range(HALF):
            span = lanes(first + j)
            grad_scaled = (own_ref[span, :] + got_ref[span, :].astype(F32)).T
            mixed = mixed_ref[:, span]
            inv_rms = lax.rsqrt(jnp.mean(mixed * mixed, axis=-1, keepdims=True) + EPSILON)
            normed = mixed * inv_rms
            g = grad_scaled * gain_ref[:, span]
            low = (inv_rms * (g - normed * jnp.mean(g * normed, axis=-1, keepdims=True))).astype(BF16)
            low_ref[:, span] = low
            head_queries = jnp.where(head_rows, queries_ref[:, span], 0)
            ref[j] = dot(head_queries, low, TN).astype(BF16)


def grad_mixed_part(lengths, own, got, mixed, gain, queries):
    half = jax.ShapeDtypeStruct((HALF, HEAD_DIM, HEAD_DIM), BF16)
    return pl.pallas_call(
        grad_mixed_kernel,
        out_shape=(jax.ShapeDtypeStruct((TOK, DI), BF16), half, half),
        in_specs=[SMEM] + [VMEM] * 5,
        out_specs=(VMEM,) * 3,
        compiler_params=params(),
        cost_estimate=cost(60_000_000, 4_000_000),
        name="grad_mixed_part",
    )(lengths, own, got, mixed, gain, queries)


def output_kernel(scaled_ref, scaled_got_ref, *refs):
    pieces, (own_ref, give_ref, both_ref, weight_ref) = refs[:Y], refs[Y:]
    for step, piece in enumerate(pieces):
        weight_ref[shard_rows(step), :] = piece[...]
    both_ref[:TOK] = scaled_ref[...]
    both_ref[TOK:] = scaled_got_ref[...]
    for start in range(0, D // 2, 256):
        block = dot(both_ref[...], weight_ref[:, start : start + 256], NN).astype(BF16)
        own_ref[:, start : start + 256] = block[:TOK]
        give_ref[:, start : start + 256] = block[TOK:]


def output_part(scaled, scaled_got, pieces):
    half = jax.ShapeDtypeStruct((TOK, D // 2), BF16)
    return pl.pallas_call(
        output_kernel,
        out_shape=(half, half),
        in_specs=[VMEM] * (2 + Y),
        out_specs=(VMEM, VMEM),
        scratch_shapes=[pltpu.VMEM((2 * TOK, DI), BF16), pltpu.VMEM((DI, D // 2), BF16)],
        compiler_params=params(),
        cost_estimate=cost(810_000_000, 5_000_000),
        name="output_part",
    )(scaled, scaled_got, *pieces)


def grads_kernel(
    lengths_ref, queries_ref, keys_ref, values_ref, low_ref, attn_ref, mine_ref, other_ref,
    dq_ref, dk_ref, dv_ref,
):
    chip, core = chip_and_core()
    ends = running_ends(lengths_ref)
    start = (chip * 2 + core) * TOK
    mask = same_doc_mask(ends, start)
    carry = rows_of(start) < next_end(ends, start - 1)
    for part, ref in ((0, mine_ref), (1, other_ref)):
        first = HALF * core if part == 0 else HALF * (1 - core)
        for j in range(HALF):
            span = lanes(first + j)
            low = low_ref[:, span]
            queries = queries_ref[:, span]
            grad_attn = jnp.where(mask, dot(low, values_ref[:, span], NT), 0.0).astype(BF16)
            from_state = jnp.where(carry, dot(low, ref[j], NT), 0.0)
            dq_ref[:, span] = (dot(grad_attn, keys_ref[:, span], NN) + from_state).astype(BF16)
            dk_ref[:, span] = dot(grad_attn, queries, TN)
            dv_ref[:, span] = dot(attn_ref[first + j], low, TN)


def grads_part(lengths, queries, keys, values, low, attn, mine, other):
    full = jax.ShapeDtypeStruct((TOK, DI), F32)
    return pl.pallas_call(
        grads_kernel,
        out_shape=(jax.ShapeDtypeStruct((TOK, DI), BF16), full, full),
        in_specs=[SMEM] + [VMEM] * 7,
        out_specs=(VMEM,) * 3,
        compiler_params=params(),
        cost_estimate=cost(250_000_000, 5_000_000),
        name="grads_part",
    )(lengths, queries, keys, values, low, attn, mine, other)


def last_kernel(
    lengths_ref, keys_ref, values_ref, dk_part_ref, dv_part_ref, out_own_ref, out_got_ref, mine_ref, other_ref,
    dk_ref, dv_ref, output_ref,
):
    chip, core = chip_and_core()
    width = D // 2
    output_ref[:, pl.ds(pl.multiple_of(core * width, width), width)] = out_own_ref[...]
    output_ref[:, pl.ds(pl.multiple_of((1 - core) * width, width), width)] = out_got_ref[...]
    ends = running_ends(lengths_ref)
    start = (chip * 2 + core) * TOK
    after = rows_of(start) >= last_end(ends, start + TOK)
    for part, ref in ((0, mine_ref), (1, other_ref)):
        first = HALF * core if part == 0 else HALF * (1 - core)
        for j in range(HALF):
            span = lanes(first + j)
            state = ref[j]
            from_keys = jnp.where(after, dot(values_ref[:, span], state, NT), 0.0)
            dk_ref[:, span] = (dk_part_ref[:, span] + from_keys).astype(BF16)
            from_values = jnp.where(after, dot(keys_ref[:, span], state, NN), 0.0)
            dv_ref[:, span] = (dv_part_ref[:, span] + from_values).astype(BF16)


def last_part(lengths, keys, values, dk, dv, out_own, out_got, mine, other):
    full = jax.ShapeDtypeStruct((TOK, DI), BF16)
    return pl.pallas_call(
        last_kernel,
        out_shape=(full, full, jax.ShapeDtypeStruct((TOK, D), BF16)),
        in_specs=[SMEM] + [VMEM] * 8,
        out_specs=(VMEM,) * 3,
        compiler_params=params(),
        cost_estimate=cost(100_000_000, 4_500_000),
        name="last_part",
    )(lengths, keys, values, dk, dv, out_own, out_got, mine, other)


def swap_cores(block):
    return lax.ppermute(block, "core", [(0, 1), (1, 0)])


def from_chip(block, distance):
    chips = range(CHIPS)
    pairs = [(2 * (i - distance) + c, 2 * i + c) for i in chips for c in range(2) if i - distance in chips]
    return lax.ppermute(block, ("z", "x", "core"), pairs)


def along_y(block):
    pairs = [(i, (i + 1) % Y) for i in range(Y)] + [(Y + i, Y + (i - 1) % Y) for i in range(Y)]
    return lax.ppermute(block, ("core", "fsdp"), pairs)


def window(keep, give, coef, sign):
    def row(index):
        return coef[index + (0 if sign > 0 else BACK)]

    got = swap_cores(give).astype(F32)
    own = keep.astype(F32)
    chip_sum = (row(CA) * own + row(CB) * got).astype(BF16)
    if sign > 0:
        before = from_chip(chip_sum, sign)
        pair_sum = (chip_sum.astype(F32) + row(MP) * before.astype(F32)).astype(BF16)
        near = from_chip(pair_sum, sign)
        far = from_chip(pair_sum, 3 * sign)
        enter = row(ME1) * near.astype(F32) + row(ME3) * far.astype(F32)
    else:
        sums = []
        for chips in (1, 2, 3, 4):
            sums.append(from_chip(chip_sum, chips * sign).astype(F32))
        enter = row(ME1) * sums[0] + coef[BACK_2] * sums[1] + row(ME3) * sums[2] + coef[BACK_4] * sums[3]
    other = swap_cores((row(CS) * own + row(ES) * enter).astype(BF16))
    mine = (row(CR) * got + row(ER) * enter).astype(BF16)
    return mine, other


def layer(queries, keys, values, lengths, gain, out_weight, cotangent):
    queries, keys, values, cotangent = queries[0], keys[0], values[0], cotangent[0]
    gain_row = gain.reshape(1, DI)
    half, cot_keep, cot_give = take_half(out_weight, cotangent)
    pieces = [half]
    for _ in range(1, Y):
        pieces.append(along_y(pieces[-1]))
    cot_got = swap_cores(cot_give)

    keep, give, coef = local_state(lengths, keys, values)
    mine, other = window(keep, give, coef, 1)
    attn, inside = inside_part(lengths, queries, keys, values)
    mixed, scaled = mixed_part(lengths, queries, inside, mine, other, gain_row)
    scaled_got = swap_cores(scaled)
    own_share, give_share = share_part(cot_keep, cot_got, pieces[:-1])
    own_share, give_share = share_end(cot_keep, cot_got, pieces[-1], own_share, give_share)
    got_share = swap_cores(give_share)
    low, give_back, keep_back = grad_mixed_part(lengths, own_share, got_share, mixed, gain_row, queries)
    back_mine, back_other = window(keep_back, give_back, coef, -1)
    out_own, out_give = output_part(scaled, scaled_got, pieces)
    out_got = swap_cores(out_give)
    dq, dk_part, dv_part = grads_part(lengths, queries, keys, values, low, attn, mine, other)
    dk, dv, output = last_part(lengths, keys, values, dk_part, dv_part, out_own, out_got, back_mine, back_other)
    return output[None], dq[None], dk[None], dv[None]


def solution(mesh):
    split = Mesh(mesh.devices.reshape(8, 4, 2, 8), ("z", "x", "core", "fsdp"))
    tokens = P("fsdp", ("z", "x", "core"), None)
    return jax.shard_map(
        layer,
        mesh=split,
        in_specs=(tokens, tokens, tokens, P("fsdp", None), P(), P("fsdp", None), tokens),
        out_specs=(tokens,) * 4,
        check_vma=False,
    )
```

```python
import jax
import jax.numpy as jnp
from jax import lax
from jax.experimental import pallas as pl
from jax.experimental.pallas import tpu as pltpu
from jax.sharding import Mesh, PartitionSpec as P


HEADS = 12
HALF = 6
HEAD_DIM = 128
NDOCS = 16
TOK = 128
SHARD = 192
Y = 8
DI = HEADS * HEAD_DIM
D = 2048
CHIPS = 32
EPSILON = 1.0
F32 = jnp.float32
BF16 = jnp.bfloat16

CA, CB, MP, ME1, ME3, CS, ES, CR, ER = range(9)
BACK = 9
BACK_2, BACK_4 = 18, 19
ROWS = 24

VMEM = pl.BlockSpec(memory_space=pltpu.VMEM)
SMEM = pl.BlockSpec(memory_space=pltpu.SMEM)
HBM = pl.BlockSpec(memory_space=pltpu.HBM)


def params(mib=24):
    return pltpu.CompilerParams(vmem_limit_bytes=mib << 20)


def cost(flops, moved):
    return pl.CostEstimate(flops=flops, bytes_accessed=moved, transcendentals=0)


def chip_and_core():
    return lax.axis_index("z") * 4 + lax.axis_index("x"), lax.axis_index("core")


def running_ends(lengths_ref):
    ends, total = [], jnp.int32(0)
    for j in range(NDOCS):
        total = total + lengths_ref[0, j]
        ends.append(total)
    return ends


def last_end(ends, position):
    best = jnp.int32(-(1 << 30))
    for end in ends:
        best = jnp.where(end <= position, end, best)
    return best


def next_end(ends, position):
    best = jnp.int32(1 << 30)
    for end in reversed(ends):
        best = jnp.where(end > position, end, best)
    return best


def same(ends, early, late):
    return last_end(ends, late) <= early


def lanes(head):
    start = head * HEAD_DIM
    return pl.ds(start if isinstance(head, int) else pl.multiple_of(start, HEAD_DIM), HEAD_DIM)


def dot(a, b, contract):
    return lax.dot_general(a, b, ((contract[0], contract[1]), ((), ())), preferred_element_type=F32)


NN = ((1,), (0,))
NT = ((1,), (1,))
TN = ((0,), (0,))


def rows_of(start, width=HEAD_DIM):
    return start + lax.broadcasted_iota(jnp.int32, (TOK, width), 0)


def same_doc_mask(ends, start):
    rows = rows_of(start)
    columns = start + lax.broadcasted_iota(jnp.int32, (TOK, TOK), 1)
    first = jnp.full((TOK, TOK), -(1 << 30), jnp.int32)
    for end in ends:
        first = jnp.where(end <= rows, end, first)
    return (columns <= rows) & (columns >= first)


def take_half_kernel(weight_ref, cot_ref, half_ref, cot_keep_ref, cot_give_ref, sems):
    _, core = chip_and_core()
    width = D // 2
    mine = pl.ds(pl.multiple_of(core * width, width), width)
    theirs = pl.ds(pl.multiple_of((1 - core) * width, width), width)
    copies = [
        pltpu.make_async_copy(weight_ref.at[:, mine], half_ref, sems.at[0]),
        pltpu.make_async_copy(cot_ref.at[:, theirs], cot_give_ref, sems.at[1]),
        pltpu.make_async_copy(cot_ref.at[:, mine], cot_keep_ref, sems.at[2]),
    ]
    for copy in copies:
        copy.start()
    for copy in copies:
        copy.wait()


def take_half(weight, cotangent):
    cot = jax.ShapeDtypeStruct((TOK, D // 2), BF16)
    return pl.pallas_call(
        take_half_kernel,
        out_shape=(jax.ShapeDtypeStruct((SHARD, D // 2), BF16), cot, cot),
        in_specs=[HBM, HBM],
        out_specs=(VMEM, VMEM, VMEM),
        scratch_shapes=[pltpu.SemaphoreType.DMA((3,))],
        compiler_params=params(60),
        cost_estimate=cost(1000, 2_000_000),
        name="take_half",
    )(weight, cotangent)


def local_state_kernel(
    lengths_ref, keys_hbm, values_hbm, keep_ref, give_ref, coef_ref, keys_ref, values_ref, sems
):
    copies = [
        pltpu.make_async_copy(keys_hbm, keys_ref, sems.at[0]),
        pltpu.make_async_copy(values_hbm, values_ref, sems.at[1]),
    ]
    for copy in copies:
        copy.start()
    for copy in copies:
        copy.wait()
    chip, core = chip_and_core()
    ends = running_ends(lengths_ref)
    start = (chip * 2 + core) * TOK
    tail = rows_of(start) >= last_end(ends, start + TOK - 1)
    for part, ref in ((0, keep_ref), (1, give_ref)):
        first = HALF * core if part == 0 else HALF * (1 - core)
        for j in range(HALF):
            span = lanes(first + j)
            tail_values = jnp.where(tail, values_ref[:, span], 0)
            ref[j] = dot(keys_ref[:, span], tail_values, TN).astype(BF16)
    base = chip * 2 * TOK
    one, zero = jnp.float32(1), jnp.float32(0)

    def flag(condition):
        return jnp.where(condition, one, zero)

    def put(row, value):
        coef_ref[row : row + 1, :] = jnp.full((1, 128), value, F32)

    low = core == 0
    inner = flag(same(ends, base + 127, base + 255))
    across = flag(same(ends, base - 1, base + 127))
    put(CA, jnp.where(low, inner, one))
    put(CB, jnp.where(low, one, inner))
    put(MP, flag((chip >= 1) & same(ends, base - 1, base + 255)))
    put(ME1, flag(chip >= 1))
    put(ME3, flag((chip >= 3) & same(ends, base - 513, base - 1)))
    put(CS, jnp.where(low, one, zero))
    put(ES, jnp.where(low, across, one))
    put(CR, jnp.where(low, zero, one))
    put(ER, jnp.where(low, one, across))
    inner = flag(same(ends, base, base + 128))
    across = flag(same(ends, base + 128, base + 256))
    put(BACK + CA, jnp.where(low, one, inner))
    put(BACK + CB, jnp.where(low, inner, one))
    put(BACK + MP, flag((chip <= CHIPS - 2) & same(ends, base, base + 256)))
    put(BACK + ME1, flag(chip <= CHIPS - 2))
    put(BACK + ME3, flag((chip <= CHIPS - 4) & same(ends, base + 256, base + 768)))
    put(BACK + CS, jnp.where(low, zero, one))
    put(BACK + ES, jnp.where(low, one, across))
    put(BACK + CR, jnp.where(low, one, zero))
    put(BACK + ER, jnp.where(low, across, one))
    put(BACK_2, flag((chip <= CHIPS - 3) & same(ends, base + 256, base + 512)))
    put(BACK_4, flag((chip <= CHIPS - 5) & same(ends, base + 256, base + 1024)))
    for row in range(BACK_4 + 1, ROWS):
        put(row, zero)


def local_state(lengths, keys, values):
    half = jax.ShapeDtypeStruct((HALF, HEAD_DIM, HEAD_DIM), BF16)
    return pl.pallas_call(
        local_state_kernel,
        out_shape=(half, half, jax.ShapeDtypeStruct((ROWS, 128), F32)),
        in_specs=[SMEM, HBM, HBM],
        out_specs=(VMEM, VMEM, VMEM),
        scratch_shapes=[
            pltpu.VMEM((TOK, DI), BF16),
            pltpu.VMEM((TOK, DI), BF16),
            pltpu.SemaphoreType.DMA((2,)),
        ],
        compiler_params=params(),
        cost_estimate=cost(50_000_000, 1_200_000),
        name="local_state",
    )(lengths, keys, values)


def inside_kernel(lengths_ref, queries_ref, keys_ref, values_ref, attn_ref, inside_ref):
    chip, core = chip_and_core()
    ends = running_ends(lengths_ref)
    start = (chip * 2 + core) * TOK
    mask = same_doc_mask(ends, start)
    for h in range(HEADS):
        span = lanes(h)
        scores = dot(queries_ref[:, span], keys_ref[:, span], NT)
        attn = jnp.where(mask, scores, 0.0).astype(BF16)
        attn_ref[h] = attn
        inside_ref[:, span] = dot(attn, values_ref[:, span], NN)


def inside_part(lengths, queries, keys, values):
    return pl.pallas_call(
        inside_kernel,
        out_shape=(
            jax.ShapeDtypeStruct((HEADS, TOK, TOK), BF16),
            jax.ShapeDtypeStruct((TOK, DI), F32),
        ),
        in_specs=[SMEM, VMEM, VMEM, VMEM],
        out_specs=(VMEM, VMEM),
        compiler_params=params(),
        cost_estimate=cost(100_000_000, 2_400_000),
        name="inside_part",
    )(lengths, queries, keys, values)


def mixed_kernel(lengths_ref, queries_ref, inside_ref, mine_ref, other_ref, gain_ref, mixed_ref, scaled_ref):
    chip, core = chip_and_core()
    ends = running_ends(lengths_ref)
    start = (chip * 2 + core) * TOK
    carry = rows_of(start) < next_end(ends, start - 1)
    for part, ref in ((0, mine_ref), (1, other_ref)):
        first = HALF * core if part == 0 else HALF * (1 - core)
        for j in range(HALF):
            span = lanes(first + j)
            carried = dot(queries_ref[:, span], ref[j], NN)
            mixed = inside_ref[:, span] + jnp.where(carry, carried, 0.0)
            mixed_ref[:, span] = mixed
            inv_rms = lax.rsqrt(jnp.mean(mixed * mixed, axis=-1, keepdims=True) + EPSILON)
            scaled_ref[:, span] = (mixed * inv_rms * gain_ref[:, span]).astype(BF16)


def mixed_part(lengths, queries, inside, mine, other, gain):
    return pl.pallas_call(
        mixed_kernel,
        out_shape=(jax.ShapeDtypeStruct((TOK, DI), F32), jax.ShapeDtypeStruct((TOK, DI), BF16)),
        in_specs=[SMEM, VMEM, VMEM, VMEM, VMEM, VMEM],
        out_specs=(VMEM, VMEM),
        compiler_params=params(),
        cost_estimate=cost(50_000_000, 2_700_000),
        name="mixed_part",
    )(lengths, queries, inside, mine, other, gain)


HELD = ((0, 1), (-1, -2), (2, 3), (-3, -4))


def shard_rows(offset):
    y = lax.axis_index("fsdp")
    way = 1 - 2 * lax.rem(y + lax.axis_index("core"), 2)
    owner = lax.rem(y + Y + way * offset, Y)
    return pl.ds(pl.multiple_of(owner * SHARD, 64), SHARD)


def add_share(held, block_ref, cot_ref, own_ref, give_ref):
    for number, offset in enumerate(held):
        share = dot(block_ref[number * SHARD : (number + 1) * SHARD], cot_ref[...], NT)
        rows = shard_rows(offset)
        own_ref[rows, :] = share[:, :TOK]
        give_ref[rows, :] = share[:, TOK:].astype(BF16)


def share_kernel(cot_keep_ref, cot_got_ref, *refs):
    blocks, (own_ref, give_ref, cot_ref) = refs[:3], refs[3:]
    cot_ref[:TOK] = cot_keep_ref[...]
    cot_ref[TOK:] = cot_got_ref[...]
    for held, block_ref in zip(HELD, blocks):
        add_share(held, block_ref, cot_ref, own_ref, give_ref)


SHARE_SHAPES = (jax.ShapeDtypeStruct((DI, TOK), F32), jax.ShapeDtypeStruct((DI, TOK), BF16))


def share_part(cot_keep, cot_got, blocks):
    return pl.pallas_call(
        share_kernel,
        out_shape=SHARE_SHAPES,
        in_specs=[VMEM] * 5,
        out_specs=(VMEM, VMEM),
        scratch_shapes=[pltpu.VMEM((2 * TOK, D // 2), BF16)],
        compiler_params=params(),
        cost_estimate=cost(700_000_000, 4_500_000),
        name="share_part",
    )(cot_keep, cot_got, *blocks)


def share_end_kernel(
    cot_keep_ref, cot_got_ref, block_ref, own_in_ref, give_in_ref, own_ref, give_ref, cot_ref
):
    cot_ref[:TOK] = cot_keep_ref[...]
    cot_ref[TOK:] = cot_got_ref[...]
    own_ref[...] = own_in_ref[...]
    give_ref[...] = give_in_ref[...]
    add_share(HELD[3], block_ref, cot_ref, own_ref, give_ref)


def share_end(cot_keep, cot_got, block, own, give):
    return pl.pallas_call(
        share_end_kernel,
        out_shape=SHARE_SHAPES,
        in_specs=[VMEM] * 5,
        out_specs=(VMEM, VMEM),
        scratch_shapes=[pltpu.VMEM((2 * TOK, D // 2), BF16)],
        compiler_params=params(),
        cost_estimate=cost(100_000_000, 3_500_000),
        name="share_end",
    )(cot_keep, cot_got, block, own, give)


def grad_mixed_kernel(
    lengths_ref, own_ref, got_ref, mixed_ref, gain_ref, queries_ref, low_ref, give_ref, keep_ref
):
    chip, core = chip_and_core()
    ends = running_ends(lengths_ref)
    start = (chip * 2 + core) * TOK
    head_rows = rows_of(start) < next_end(ends, start)
    for part, ref in ((0, give_ref), (1, keep_ref)):
        first = HALF * (1 - core) if part == 0 else HALF * core
        for j in range(HALF):
            span = lanes(first + j)
            grad_scaled = (own_ref[span, :] + got_ref[span, :].astype(F32)).T
            mixed = mixed_ref[:, span]
            inv_rms = lax.rsqrt(jnp.mean(mixed * mixed, axis=-1, keepdims=True) + EPSILON)
            normed = mixed * inv_rms
            g = grad_scaled * gain_ref[:, span]
            low = (inv_rms * (g - normed * jnp.mean(g * normed, axis=-1, keepdims=True))).astype(BF16)
            low_ref[:, span] = low
            head_queries = jnp.where(head_rows, queries_ref[:, span], 0)
            ref[j] = dot(head_queries, low, TN).astype(BF16)


def grad_mixed_part(lengths, own, got, mixed, gain, queries):
    half = jax.ShapeDtypeStruct((HALF, HEAD_DIM, HEAD_DIM), BF16)
    return pl.pallas_call(
        grad_mixed_kernel,
        out_shape=(jax.ShapeDtypeStruct((TOK, DI), BF16), half, half),
        in_specs=[SMEM] + [VMEM] * 5,
        out_specs=(VMEM,) * 3,
        compiler_params=params(),
        cost_estimate=cost(60_000_000, 4_000_000),
        name="grad_mixed_part",
    )(lengths, own, got, mixed, gain, queries)


def output_kernel(scaled_ref, scaled_got_ref, *refs):
    blocks, (own_ref, give_ref, both_ref, weight_ref) = refs[:4], refs[4:]
    for held, block_ref in zip(HELD, blocks):
        for number, offset in enumerate(held):
            weight_ref[shard_rows(offset), :] = block_ref[number * SHARD : (number + 1) * SHARD]
    both_ref[:TOK] = scaled_ref[...]
    both_ref[TOK:] = scaled_got_ref[...]
    for start in range(0, D // 2, 256):
        block = dot(both_ref[...], weight_ref[:, start : start + 256], NN).astype(BF16)
        own_ref[:, start : start + 256] = block[:TOK]
        give_ref[:, start : start + 256] = block[TOK:]


def output_part(scaled, scaled_got, blocks):
    half = jax.ShapeDtypeStruct((TOK, D // 2), BF16)
    return pl.pallas_call(
        output_kernel,
        out_shape=(half, half),
        in_specs=[VMEM] * 6,
        out_specs=(VMEM, VMEM),
        scratch_shapes=[pltpu.VMEM((2 * TOK, DI), BF16), pltpu.VMEM((DI, D // 2), BF16)],
        compiler_params=params(),
        cost_estimate=cost(810_000_000, 5_000_000),
        name="output_part",
    )(scaled, scaled_got, *blocks)


def grads_kernel(
    lengths_ref, queries_ref, keys_ref, values_ref, low_ref, attn_ref, mine_ref, other_ref,
    dq_ref, dk_ref, dv_ref,
):
    chip, core = chip_and_core()
    ends = running_ends(lengths_ref)
    start = (chip * 2 + core) * TOK
    mask = same_doc_mask(ends, start)
    carry = rows_of(start) < next_end(ends, start - 1)
    for part, ref in ((0, mine_ref), (1, other_ref)):
        first = HALF * core if part == 0 else HALF * (1 - core)
        for j in range(HALF):
            span = lanes(first + j)
            low = low_ref[:, span]
            queries = queries_ref[:, span]
            grad_attn = jnp.where(mask, dot(low, values_ref[:, span], NT), 0.0).astype(BF16)
            from_state = jnp.where(carry, dot(low, ref[j], NT), 0.0)
            dq_ref[:, span] = (dot(grad_attn, keys_ref[:, span], NN) + from_state).astype(BF16)
            dk_ref[:, span] = dot(grad_attn, queries, TN)
            dv_ref[:, span] = dot(attn_ref[first + j], low, TN)


def grads_part(lengths, queries, keys, values, low, attn, mine, other):
    full = jax.ShapeDtypeStruct((TOK, DI), F32)
    return pl.pallas_call(
        grads_kernel,
        out_shape=(jax.ShapeDtypeStruct((TOK, DI), BF16), full, full),
        in_specs=[SMEM] + [VMEM] * 7,
        out_specs=(VMEM,) * 3,
        compiler_params=params(),
        cost_estimate=cost(250_000_000, 5_000_000),
        name="grads_part",
    )(lengths, queries, keys, values, low, attn, mine, other)


def last_kernel(
    lengths_ref, keys_ref, values_ref, dk_part_ref, dv_part_ref, out_own_ref, out_got_ref, mine_ref, other_ref,
    dk_ref, dv_ref, output_ref,
):
    chip, core = chip_and_core()
    width = D // 2
    output_ref[:, pl.ds(pl.multiple_of(core * width, width), width)] = out_own_ref[...]
    output_ref[:, pl.ds(pl.multiple_of((1 - core) * width, width), width)] = out_got_ref[...]
    ends = running_ends(lengths_ref)
    start = (chip * 2 + core) * TOK
    after = rows_of(start) >= last_end(ends, start + TOK)
    for part, ref in ((0, mine_ref), (1, other_ref)):
        first = HALF * core if part == 0 else HALF * (1 - core)
        for j in range(HALF):
            span = lanes(first + j)
            state = ref[j]
            from_keys = jnp.where(after, dot(values_ref[:, span], state, NT), 0.0)
            dk_ref[:, span] = (dk_part_ref[:, span] + from_keys).astype(BF16)
            from_values = jnp.where(after, dot(keys_ref[:, span], state, NN), 0.0)
            dv_ref[:, span] = (dv_part_ref[:, span] + from_values).astype(BF16)


def last_part(lengths, keys, values, dk, dv, out_own, out_got, mine, other):
    full = jax.ShapeDtypeStruct((TOK, DI), BF16)
    return pl.pallas_call(
        last_kernel,
        out_shape=(full, full, jax.ShapeDtypeStruct((TOK, D), BF16)),
        in_specs=[SMEM] + [VMEM] * 8,
        out_specs=(VMEM,) * 3,
        compiler_params=params(),
        cost_estimate=cost(100_000_000, 4_500_000),
        name="last_part",
    )(lengths, keys, values, dk, dv, out_own, out_got, mine, other)


def swap_cores(block):
    return lax.ppermute(block, "core", [(0, 1), (1, 0)])


def from_chip(block, distance):
    chips = range(CHIPS)
    pairs = [(2 * (i - distance) + c, 2 * i + c) for i in chips for c in range(2) if i - distance in chips]
    return lax.ppermute(block, ("z", "x", "core"), pairs)


def exchange(block, sense):
    pairs = []
    for core in range(2):
        for y in range(Y):
            way = 1 - 2 * ((y + core) % 2)
            pairs.append((core * Y + y, core * Y + (y + sense * way) % Y))
    return lax.ppermute(block, ("core", "fsdp"), pairs)


def window(keep, give, coef, sign):
    def row(index):
        return coef[index + (0 if sign > 0 else BACK)]

    got = swap_cores(give).astype(F32)
    own = keep.astype(F32)
    chip_sum = (row(CA) * own + row(CB) * got).astype(BF16)
    if sign > 0:
        before = from_chip(chip_sum, sign)
        pair_sum = (chip_sum.astype(F32) + row(MP) * before.astype(F32)).astype(BF16)
        near = from_chip(pair_sum, sign)
        far = from_chip(pair_sum, 3 * sign)
        enter = row(ME1) * near.astype(F32) + row(ME3) * far.astype(F32)
    else:
        sums = []
        for chips in (1, 2, 3, 4):
            sums.append(from_chip(chip_sum, chips * sign).astype(F32))
        enter = row(ME1) * sums[0] + coef[BACK_2] * sums[1] + row(ME3) * sums[2] + coef[BACK_4] * sums[3]
    other = swap_cores((row(CS) * own + row(ES) * enter).astype(BF16))
    mine = (row(CR) * got + row(ER) * enter).astype(BF16)
    return mine, other


def layer(queries, keys, values, lengths, gain, out_weight, cotangent):
    queries, keys, values, cotangent = queries[0], keys[0], values[0], cotangent[0]
    gain_row = gain.reshape(1, DI)
    half, cot_keep, cot_give = take_half(out_weight, cotangent)
    got_half = exchange(half, 1)
    blocks = [jnp.concatenate([half, got_half], axis=0)]
    for sense in (-1, 1, -1):
        blocks.append(exchange(blocks[-1], sense))
    cot_got = swap_cores(cot_give)

    keep, give, coef = local_state(lengths, keys, values)
    mine, other = window(keep, give, coef, 1)
    attn, inside = inside_part(lengths, queries, keys, values)
    mixed, scaled = mixed_part(lengths, queries, inside, mine, other, gain_row)
    scaled_got = swap_cores(scaled)
    own_share, give_share = share_part(cot_keep, cot_got, blocks[:3])
    own_share, give_share = share_end(cot_keep, cot_got, blocks[3], own_share, give_share)
    got_share = swap_cores(give_share)
    low, give_back, keep_back = grad_mixed_part(lengths, own_share, got_share, mixed, gain_row, queries)
    back_mine, back_other = window(keep_back, give_back, coef, -1)
    out_own, out_give = output_part(scaled, scaled_got, blocks)
    out_got = swap_cores(out_give)
    dq, dk_part, dv_part = grads_part(lengths, queries, keys, values, low, attn, mine, other)
    dk, dv, output = last_part(lengths, keys, values, dk_part, dv_part, out_own, out_got, back_mine, back_other)
    return output[None], dq[None], dk[None], dv[None]


def solution(mesh):
    split = Mesh(mesh.devices.reshape(8, 4, 2, 8), ("z", "x", "core", "fsdp"))
    tokens = P("fsdp", ("z", "x", "core"), None)
    return jax.shard_map(
        layer,
        mesh=split,
        in_specs=(tokens, tokens, tokens, P("fsdp", None), P(), P("fsdp", None), tokens),
        out_specs=(tokens,) * 4,
        check_vma=False,
    )
```

```python
import jax
import jax.numpy as jnp
from jax import lax
from jax.experimental import pallas as pl
from jax.experimental.pallas import tpu as pltpu
from jax.sharding import Mesh, PartitionSpec as P


HEADS = 12
HALF = 6
HEAD_DIM = 128
NDOCS = 16
TOK = 128
SHARD = 192
Y = 8
DI = HEADS * HEAD_DIM
D = 2048
CHIPS = 32
EPSILON = 1.0
F32 = jnp.float32
BF16 = jnp.bfloat16

CA, CB, MP, ME1, ME3, CS, ES, CR, ER = range(9)
BACK = 9
ROWS = 24

VMEM = pl.BlockSpec(memory_space=pltpu.VMEM)
SMEM = pl.BlockSpec(memory_space=pltpu.SMEM)
HBM = pl.BlockSpec(memory_space=pltpu.HBM)


def params(mib=24):
    return pltpu.CompilerParams(vmem_limit_bytes=mib << 20)


def cost(flops, moved):
    return pl.CostEstimate(flops=flops, bytes_accessed=moved, transcendentals=0)


def chip_and_core():
    return lax.axis_index("z") * 4 + lax.axis_index("x"), lax.axis_index("core")


def running_ends(lengths_ref):
    ends, total = [], jnp.int32(0)
    for j in range(NDOCS):
        total = total + lengths_ref[0, j]
        ends.append(total)
    return ends


def last_end(ends, position):
    best = jnp.int32(-(1 << 30))
    for end in ends:
        best = jnp.where(end <= position, end, best)
    return best


def next_end(ends, position):
    best = jnp.int32(1 << 30)
    for end in reversed(ends):
        best = jnp.where(end > position, end, best)
    return best


def same(ends, early, late):
    return last_end(ends, late) <= early


def lanes(head):
    start = head * HEAD_DIM
    return pl.ds(start if isinstance(head, int) else pl.multiple_of(start, HEAD_DIM), HEAD_DIM)


def dot(a, b, contract):
    return lax.dot_general(a, b, ((contract[0], contract[1]), ((), ())), preferred_element_type=F32)


NN = ((1,), (0,))
NT = ((1,), (1,))
TN = ((0,), (0,))


def rows_of(start, width=HEAD_DIM):
    return start + lax.broadcasted_iota(jnp.int32, (TOK, width), 0)


def same_doc_mask(ends, start):
    rows = rows_of(start)
    columns = start + lax.broadcasted_iota(jnp.int32, (TOK, TOK), 1)
    first = jnp.full((TOK, TOK), -(1 << 30), jnp.int32)
    for end in ends:
        first = jnp.where(end <= rows, end, first)
    return (columns <= rows) & (columns >= first)


def take_half_kernel(weight_ref, cot_ref, half_ref, cot_keep_ref, cot_give_ref, sems):
    _, core = chip_and_core()
    width = D // 2
    mine = pl.ds(pl.multiple_of(core * width, width), width)
    theirs = pl.ds(pl.multiple_of((1 - core) * width, width), width)
    copies = [
        pltpu.make_async_copy(weight_ref.at[:, mine], half_ref, sems.at[0]),
        pltpu.make_async_copy(cot_ref.at[:, theirs], cot_give_ref, sems.at[1]),
        pltpu.make_async_copy(cot_ref.at[:, mine], cot_keep_ref, sems.at[2]),
    ]
    for copy in copies:
        copy.start()
    for copy in copies:
        copy.wait()


def take_half(weight, cotangent):
    cot = jax.ShapeDtypeStruct((TOK, D // 2), BF16)
    return pl.pallas_call(
        take_half_kernel,
        out_shape=(jax.ShapeDtypeStruct((SHARD, D // 2), BF16), cot, cot),
        in_specs=[HBM, HBM],
        out_specs=(VMEM, VMEM, VMEM),
        scratch_shapes=[pltpu.SemaphoreType.DMA((3,))],
        compiler_params=params(60),
        cost_estimate=cost(1000, 2_000_000),
        name="take_half",
    )(weight, cotangent)


def local_state_kernel(
    lengths_ref, keys_hbm, values_hbm, keep_ref, give_ref, coef_ref, keys_ref, values_ref, sems
):
    copies = [
        pltpu.make_async_copy(keys_hbm, keys_ref, sems.at[0]),
        pltpu.make_async_copy(values_hbm, values_ref, sems.at[1]),
    ]
    for copy in copies:
        copy.start()
    for copy in copies:
        copy.wait()
    chip, core = chip_and_core()
    ends = running_ends(lengths_ref)
    start = (chip * 2 + core) * TOK
    tail = rows_of(start) >= last_end(ends, start + TOK - 1)
    for part, ref in ((0, keep_ref), (1, give_ref)):
        first = HALF * core if part == 0 else HALF * (1 - core)
        for j in range(HALF):
            span = lanes(first + j)
            tail_values = jnp.where(tail, values_ref[:, span], 0)
            ref[j] = dot(keys_ref[:, span], tail_values, TN).astype(BF16)
    base = chip * 2 * TOK
    one, zero = jnp.float32(1), jnp.float32(0)

    def flag(condition):
        return jnp.where(condition, one, zero)

    def put(row, value):
        coef_ref[row : row + 1, :] = jnp.full((1, 128), value, F32)

    low = core == 0
    inner = flag(same(ends, base + 127, base + 255))
    across = flag(same(ends, base - 1, base + 127))
    put(CA, jnp.where(low, inner, one))
    put(CB, jnp.where(low, one, inner))
    put(MP, flag((chip >= 1) & same(ends, base - 1, base + 255)))
    put(ME1, flag(chip >= 1))
    put(ME3, flag((chip >= 3) & same(ends, base - 513, base - 1)))
    put(CS, jnp.where(low, one, zero))
    put(ES, jnp.where(low, across, one))
    put(CR, jnp.where(low, zero, one))
    put(ER, jnp.where(low, one, across))
    inner = flag(same(ends, base, base + 128))
    across = flag(same(ends, base + 128, base + 256))
    put(BACK + CA, jnp.where(low, one, inner))
    put(BACK + CB, jnp.where(low, inner, one))
    put(BACK + MP, flag((chip <= CHIPS - 2) & same(ends, base, base + 256)))
    put(BACK + ME1, flag(chip <= CHIPS - 2))
    put(BACK + ME3, flag((chip <= CHIPS - 4) & same(ends, base + 256, base + 768)))
    put(BACK + CS, jnp.where(low, zero, one))
    put(BACK + ES, jnp.where(low, one, across))
    put(BACK + CR, jnp.where(low, one, zero))
    put(BACK + ER, jnp.where(low, across, one))
    for row in range(2 * BACK, ROWS):
        put(row, zero)


def local_state(lengths, keys, values):
    half = jax.ShapeDtypeStruct((HALF, HEAD_DIM, HEAD_DIM), BF16)
    return pl.pallas_call(
        local_state_kernel,
        out_shape=(half, half, jax.ShapeDtypeStruct((ROWS, 128), F32)),
        in_specs=[SMEM, HBM, HBM],
        out_specs=(VMEM, VMEM, VMEM),
        scratch_shapes=[
            pltpu.VMEM((TOK, DI), BF16),
            pltpu.VMEM((TOK, DI), BF16),
            pltpu.SemaphoreType.DMA((2,)),
        ],
        compiler_params=params(),
        cost_estimate=cost(50_000_000, 1_200_000),
        name="local_state",
    )(lengths, keys, values)


def inside_kernel(lengths_ref, queries_ref, keys_ref, values_ref, attn_ref, inside_ref):
    chip, core = chip_and_core()
    ends = running_ends(lengths_ref)
    start = (chip * 2 + core) * TOK
    mask = same_doc_mask(ends, start)
    for h in range(HEADS):
        span = lanes(h)
        scores = dot(queries_ref[:, span], keys_ref[:, span], NT)
        attn = jnp.where(mask, scores, 0.0).astype(BF16)
        attn_ref[h] = attn
        inside_ref[:, span] = dot(attn, values_ref[:, span], NN)


def inside_part(lengths, queries, keys, values):
    return pl.pallas_call(
        inside_kernel,
        out_shape=(
            jax.ShapeDtypeStruct((HEADS, TOK, TOK), BF16),
            jax.ShapeDtypeStruct((TOK, DI), F32),
        ),
        in_specs=[SMEM, VMEM, VMEM, VMEM],
        out_specs=(VMEM, VMEM),
        compiler_params=params(),
        cost_estimate=cost(100_000_000, 2_400_000),
        name="inside_part",
    )(lengths, queries, keys, values)


def mixed_kernel(lengths_ref, queries_ref, inside_ref, mine_ref, other_ref, gain_ref, mixed_ref, scaled_ref):
    chip, core = chip_and_core()
    ends = running_ends(lengths_ref)
    start = (chip * 2 + core) * TOK
    carry = rows_of(start) < next_end(ends, start - 1)
    for part, ref in ((0, mine_ref), (1, other_ref)):
        first = HALF * core if part == 0 else HALF * (1 - core)
        for j in range(HALF):
            span = lanes(first + j)
            carried = dot(queries_ref[:, span], ref[j], NN)
            mixed = inside_ref[:, span] + jnp.where(carry, carried, 0.0)
            mixed_ref[:, span] = mixed
            inv_rms = lax.rsqrt(jnp.mean(mixed * mixed, axis=-1, keepdims=True) + EPSILON)
            scaled_ref[:, span] = (mixed * inv_rms * gain_ref[:, span]).astype(BF16)


def mixed_part(lengths, queries, inside, mine, other, gain):
    return pl.pallas_call(
        mixed_kernel,
        out_shape=(jax.ShapeDtypeStruct((TOK, DI), F32), jax.ShapeDtypeStruct((TOK, DI), BF16)),
        in_specs=[SMEM, VMEM, VMEM, VMEM, VMEM, VMEM],
        out_specs=(VMEM, VMEM),
        compiler_params=params(),
        cost_estimate=cost(50_000_000, 2_700_000),
        name="mixed_part",
    )(lengths, queries, inside, mine, other, gain)


HELD = ((0, 1), (-1, -2), (2, 3), (-3, -4))


def shard_rows(offset):
    y = lax.axis_index("fsdp")
    way = 1 - 2 * lax.rem(y + lax.axis_index("core"), 2)
    owner = lax.rem(y + Y + way * offset, Y)
    return pl.ds(pl.multiple_of(owner * SHARD, 64), SHARD)


def add_share(held, block_ref, cot_ref, own_ref, give_ref):
    for number, offset in enumerate(held):
        share = dot(block_ref[number * SHARD : (number + 1) * SHARD], cot_ref[...], NT)
        rows = shard_rows(offset)
        own_ref[rows, :] = share[:, :TOK]
        give_ref[rows, :] = share[:, TOK:].astype(BF16)


def share_kernel(cot_keep_ref, cot_got_ref, *refs):
    blocks, (own_ref, give_ref, cot_ref) = refs[:3], refs[3:]
    cot_ref[:TOK] = cot_keep_ref[...]
    cot_ref[TOK:] = cot_got_ref[...]
    for held, block_ref in zip(HELD, blocks):
        add_share(held, block_ref, cot_ref, own_ref, give_ref)


SHARE_SHAPES = (jax.ShapeDtypeStruct((DI, TOK), F32), jax.ShapeDtypeStruct((DI, TOK), BF16))


def share_part(cot_keep, cot_got, blocks):
    return pl.pallas_call(
        share_kernel,
        out_shape=SHARE_SHAPES,
        in_specs=[VMEM] * 5,
        out_specs=(VMEM, VMEM),
        scratch_shapes=[pltpu.VMEM((2 * TOK, D // 2), BF16)],
        compiler_params=params(),
        cost_estimate=cost(700_000_000, 4_500_000),
        name="share_part",
    )(cot_keep, cot_got, *blocks)


def share_end_kernel(
    cot_keep_ref, cot_got_ref, block_ref, own_in_ref, give_in_ref, own_ref, give_ref, cot_ref
):
    cot_ref[:TOK] = cot_keep_ref[...]
    cot_ref[TOK:] = cot_got_ref[...]
    own_ref[...] = own_in_ref[...]
    give_ref[...] = give_in_ref[...]
    add_share(HELD[3], block_ref, cot_ref, own_ref, give_ref)


def share_end(cot_keep, cot_got, block, own, give):
    return pl.pallas_call(
        share_end_kernel,
        out_shape=SHARE_SHAPES,
        in_specs=[VMEM] * 5,
        out_specs=(VMEM, VMEM),
        scratch_shapes=[pltpu.VMEM((2 * TOK, D // 2), BF16)],
        compiler_params=params(),
        cost_estimate=cost(100_000_000, 3_500_000),
        name="share_end",
    )(cot_keep, cot_got, block, own, give)


def grad_mixed_kernel(
    lengths_ref, own_ref, got_ref, mixed_ref, gain_ref, queries_ref, low_ref, give_ref, keep_ref
):
    chip, core = chip_and_core()
    ends = running_ends(lengths_ref)
    start = (chip * 2 + core) * TOK
    head_rows = rows_of(start) < next_end(ends, start)
    for part, ref in ((0, give_ref), (1, keep_ref)):
        first = HALF * (1 - core) if part == 0 else HALF * core
        for j in range(HALF):
            span = lanes(first + j)
            grad_scaled = (own_ref[span, :] + got_ref[span, :].astype(F32)).T
            mixed = mixed_ref[:, span]
            inv_rms = lax.rsqrt(jnp.mean(mixed * mixed, axis=-1, keepdims=True) + EPSILON)
            normed = mixed * inv_rms
            g = grad_scaled * gain_ref[:, span]
            low = (inv_rms * (g - normed * jnp.mean(g * normed, axis=-1, keepdims=True))).astype(BF16)
            low_ref[:, span] = low
            head_queries = jnp.where(head_rows, queries_ref[:, span], 0)
            ref[j] = dot(head_queries, low, TN).astype(BF16)


def grad_mixed_part(lengths, own, got, mixed, gain, queries):
    half = jax.ShapeDtypeStruct((HALF, HEAD_DIM, HEAD_DIM), BF16)
    return pl.pallas_call(
        grad_mixed_kernel,
        out_shape=(jax.ShapeDtypeStruct((TOK, DI), BF16), half, half),
        in_specs=[SMEM] + [VMEM] * 5,
        out_specs=(VMEM,) * 3,
        compiler_params=params(),
        cost_estimate=cost(60_000_000, 4_000_000),
        name="grad_mixed_part",
    )(lengths, own, got, mixed, gain, queries)


def output_kernel(scaled_ref, scaled_got_ref, *refs):
    blocks, (own_ref, give_ref, both_ref, weight_ref) = refs[:4], refs[4:]
    for held, block_ref in zip(HELD, blocks):
        for number, offset in enumerate(held):
            weight_ref[shard_rows(offset), :] = block_ref[number * SHARD : (number + 1) * SHARD]
    both_ref[:TOK] = scaled_ref[...]
    both_ref[TOK:] = scaled_got_ref[...]
    for start in range(0, D // 2, 256):
        block = dot(both_ref[...], weight_ref[:, start : start + 256], NN).astype(BF16)
        own_ref[:, start : start + 256] = block[:TOK]
        give_ref[:, start : start + 256] = block[TOK:]


def output_part(scaled, scaled_got, blocks):
    half = jax.ShapeDtypeStruct((TOK, D // 2), BF16)
    return pl.pallas_call(
        output_kernel,
        out_shape=(half, half),
        in_specs=[VMEM] * 6,
        out_specs=(VMEM, VMEM),
        scratch_shapes=[pltpu.VMEM((2 * TOK, DI), BF16), pltpu.VMEM((DI, D // 2), BF16)],
        compiler_params=params(),
        cost_estimate=cost(810_000_000, 5_000_000),
        name="output_part",
    )(scaled, scaled_got, *blocks)


def grads_kernel(
    lengths_ref, queries_ref, keys_ref, values_ref, low_ref, attn_ref, mine_ref, other_ref,
    dq_ref, dk_ref, dv_ref,
):
    chip, core = chip_and_core()
    ends = running_ends(lengths_ref)
    start = (chip * 2 + core) * TOK
    mask = same_doc_mask(ends, start)
    carry = rows_of(start) < next_end(ends, start - 1)
    for part, ref in ((0, mine_ref), (1, other_ref)):
        first = HALF * core if part == 0 else HALF * (1 - core)
        for j in range(HALF):
            span = lanes(first + j)
            low = low_ref[:, span]
            queries = queries_ref[:, span]
            grad_attn = jnp.where(mask, dot(low, values_ref[:, span], NT), 0.0).astype(BF16)
            from_state = jnp.where(carry, dot(low, ref[j], NT), 0.0)
            dq_ref[:, span] = (dot(grad_attn, keys_ref[:, span], NN) + from_state).astype(BF16)
            dk_ref[:, span] = dot(grad_attn, queries, TN)
            dv_ref[:, span] = dot(attn_ref[first + j], low, TN)


def grads_part(lengths, queries, keys, values, low, attn, mine, other):
    full = jax.ShapeDtypeStruct((TOK, DI), F32)
    return pl.pallas_call(
        grads_kernel,
        out_shape=(jax.ShapeDtypeStruct((TOK, DI), BF16), full, full),
        in_specs=[SMEM] + [VMEM] * 7,
        out_specs=(VMEM,) * 3,
        compiler_params=params(),
        cost_estimate=cost(250_000_000, 5_000_000),
        name="grads_part",
    )(lengths, queries, keys, values, low, attn, mine, other)


def last_kernel(
    lengths_ref, keys_ref, values_ref, dk_part_ref, dv_part_ref, out_own_ref, out_got_ref, mine_ref, other_ref,
    dk_ref, dv_ref, output_ref,
):
    chip, core = chip_and_core()
    width = D // 2
    output_ref[:, pl.ds(pl.multiple_of(core * width, width), width)] = out_own_ref[...]
    output_ref[:, pl.ds(pl.multiple_of((1 - core) * width, width), width)] = out_got_ref[...]
    ends = running_ends(lengths_ref)
    start = (chip * 2 + core) * TOK
    after = rows_of(start) >= last_end(ends, start + TOK)
    for part, ref in ((0, mine_ref), (1, other_ref)):
        first = HALF * core if part == 0 else HALF * (1 - core)
        for j in range(HALF):
            span = lanes(first + j)
            state = ref[j]
            from_keys = jnp.where(after, dot(values_ref[:, span], state, NT), 0.0)
            dk_ref[:, span] = (dk_part_ref[:, span] + from_keys).astype(BF16)
            from_values = jnp.where(after, dot(keys_ref[:, span], state, NN), 0.0)
            dv_ref[:, span] = (dv_part_ref[:, span] + from_values).astype(BF16)


def last_part(lengths, keys, values, dk, dv, out_own, out_got, mine, other):
    full = jax.ShapeDtypeStruct((TOK, DI), BF16)
    return pl.pallas_call(
        last_kernel,
        out_shape=(full, full, jax.ShapeDtypeStruct((TOK, D), BF16)),
        in_specs=[SMEM] + [VMEM] * 8,
        out_specs=(VMEM,) * 3,
        compiler_params=params(),
        cost_estimate=cost(100_000_000, 4_500_000),
        name="last_part",
    )(lengths, keys, values, dk, dv, out_own, out_got, mine, other)


def swap_cores(block):
    return lax.ppermute(block, "core", [(0, 1), (1, 0)])


def from_chip(block, distance):
    chips = range(CHIPS)
    pairs = [(2 * (i - distance) + c, 2 * i + c) for i in chips for c in range(2) if i - distance in chips]
    return lax.ppermute(block, ("z", "x", "core"), pairs)


def exchange(block, sense):
    pairs = []
    for core in range(2):
        for y in range(Y):
            way = 1 - 2 * ((y + core) % 2)
            pairs.append((core * Y + y, core * Y + (y + sense * way) % Y))
    return lax.ppermute(block, ("core", "fsdp"), pairs)


def window(keep, give, coef, sign):
    def row(index):
        return coef[index + (0 if sign > 0 else BACK)]

    got = swap_cores(give).astype(F32)
    own = keep.astype(F32)
    chip_sum = (row(CA) * own + row(CB) * got).astype(BF16)
    before = from_chip(chip_sum, sign)
    pair_sum = (chip_sum.astype(F32) + row(MP) * before.astype(F32)).astype(BF16)
    near = from_chip(pair_sum, sign)
    far = from_chip(pair_sum, 3 * sign)
    enter = row(ME1) * near.astype(F32) + row(ME3) * far.astype(F32)
    other = swap_cores((row(CS) * own + row(ES) * enter).astype(BF16))
    mine = (row(CR) * got + row(ER) * enter).astype(BF16)
    return mine, other


def layer(queries, keys, values, lengths, gain, out_weight, cotangent):
    queries, keys, values, cotangent = queries[0], keys[0], values[0], cotangent[0]
    gain_row = gain.reshape(1, DI)
    half, cot_keep, cot_give = take_half(out_weight, cotangent)
    got_half = exchange(half, 1)
    blocks = [jnp.concatenate([half, got_half], axis=0)]
    for sense in (-1, 1, -1):
        blocks.append(exchange(blocks[-1], sense))
    cot_got = swap_cores(cot_give)

    keep, give, coef = local_state(lengths, keys, values)
    mine, other = window(keep, give, coef, 1)
    attn, inside = inside_part(lengths, queries, keys, values)
    mixed, scaled = mixed_part(lengths, queries, inside, mine, other, gain_row)
    scaled_got = swap_cores(scaled)
    own_share, give_share = share_part(cot_keep, cot_got, blocks[:3])
    own_share, give_share = share_end(cot_keep, cot_got, blocks[3], own_share, give_share)
    got_share = swap_cores(give_share)
    low, give_back, keep_back = grad_mixed_part(lengths, own_share, got_share, mixed, gain_row, queries)
    back_mine, back_other = window(keep_back, give_back, coef, -1)
    out_own, out_give = output_part(scaled, scaled_got, blocks)
    out_got = swap_cores(out_give)
    dq, dk_part, dv_part = grads_part(lengths, queries, keys, values, low, attn, mine, other)
    dk, dv, output = last_part(lengths, keys, values, dk_part, dv_part, out_own, out_got, back_mine, back_other)
    return output[None], dq[None], dk[None], dv[None]


def solution(mesh):
    split = Mesh(mesh.devices.reshape(8, 4, 2, 8), ("z", "x", "core", "fsdp"))
    tokens = P("fsdp", ("z", "x", "core"), None)
    return jax.shard_map(
        layer,
        mesh=split,
        in_specs=(tokens, tokens, tokens, P("fsdp", None), P(), P("fsdp", None), tokens),
        out_specs=(tokens,) * 4,
        check_vma=False,
    )
```
